32 devices in a mesh: fsdp: 8 (over z, x), rep: 2 (over y), ctx: 2 (over core).
Axes of the slice: x: 2, y: 2, z: 4, core: 2. Of those that a mesh axis runs over, the one named last changes fastest.
Arguments:
- tokens: bfloat16 [16, 1024, 1088], P(('fsdp', 'rep'), 'ctx'), may hold values from -6 to 6
- prefix_len: int32 [16], P(('fsdp', 'rep')), may hold values from 102 to 512
- ln1_gain: bfloat16 [1088], P('fsdp'), may hold values from 0.099609375 to 1.8984375
- ln1_bias: bfloat16 [1088], P('fsdp'), may hold values from -2 to 2
- w_qkv: bfloat16 [1088, 3264], P('fsdp'), may hold values from -0.1875 to 0.1875
- b_qv: bfloat16 [2176], P('fsdp'), may hold values from -2 to 2
- w_out: bfloat16 [1088, 1088], P('fsdp'), may hold values from -3 to 3
- b_out: bfloat16 [1088], P('fsdp'), may hold values from -2 to 2
- ln2_gain: bfloat16 [1088], P('fsdp'), may hold values from 0.099609375 to 1.8984375
- ln2_bias: bfloat16 [1088], P('fsdp'), may hold values from -2 to 2
- w_up: bfloat16 [1088, 4352], P('fsdp'), may hold values from -0.1875 to 0.1875
- b_up: bfloat16 [4352], P('fsdp'), may hold values from -2 to 2
- w_down: bfloat16 [4352, 1088], P('fsdp'), may hold values from -0.125 to 0.125
- b_down: bfloat16 [1088], P('fsdp'), may hold values from -2 to 2
- cotangent: bfloat16 [16, 1024, 1088], P(('fsdp', 'rep'), 'ctx'), may hold values from -6 to 6
Outputs:
- block_out: bfloat16 [16, 1024, 1088], P(('fsdp', 'rep'), 'ctx')
- grad_tokens: float32 [16, 1024, 1088], P(('fsdp', 'rep'), 'ctx')
- grad_ln1_gain: float32 [1088], P('fsdp')
- grad_ln1_bias: float32 [1088], P('fsdp')
- grad_w_qkv: float32 [1088, 3264], P('fsdp')
- grad_b_qv: float32 [2176], P('fsdp')
- grad_w_out: float32 [1088, 1088], P('fsdp')
- grad_b_out: float32 [1088], P('fsdp')
- grad_ln2_gain: float32 [1088], P('fsdp')
- grad_ln2_bias: float32 [1088], P('fsdp')
- grad_w_up: float32 [1088, 4352], P('fsdp')
- grad_b_up: float32 [4352], P('fsdp')
- grad_w_down: float32 [4352, 1088], P('fsdp')
- grad_b_down: float32 [1088], P('fsdp')
The draws below stay inside these ranges and needn't reach their ends.
All inputs are finite; a program needn't handle non-finite values.
Results may differ from the reference program's by a relative error of at most 0.013.
Values may be sent and summed in bfloat16 or wider, within the bound.
No kernel may reach another device: no remote copies, remote signals or barrier semaphores. Data moves between devices by JAX's collectives and lax.ppermute only.
A program may use at most 192 MiB of HBM per device.

```python
import jax
import jax.numpy as jnp
from jax import lax

D = 1088
H = 17
HD = 64
FF = 4352
LEN = 1024
SEQS = 16


def touch_ends(values, stream_key, smallest, top_value):
    dims = values.shape
    spot = [jax.random.randint(jax.random.fold_in(stream_key, axis), (), 0, dims[axis]) for axis in range(len(dims))]
    values = values.at[tuple(spot)].set(smallest)
    longest = dims.index(max(dims))
    spot[longest] = (spot[longest] + 1) % dims[longest]
    return values.at[tuple(spot)].set(top_value)


def block_scale(rng, dims, shards, least, top_value):
    level = 1.0
    for axis_at, shards_of in shards:
        heights = jax.random.uniform(jax.random.fold_in(jax.random.fold_in(rng, 6), axis_at), (shards_of,), jnp.float32, least / len(shards), top_value / len(shards))
        level = level * jnp.repeat(jnp.exp(heights), dims[axis_at] // shards_of).reshape((-1,) + (1,) * (len(dims) - 1 - axis_at))
    return level


def bell_draw(stream_key, extent, spread, bound, split=(), dtype=jnp.bfloat16):
    level = block_scale(stream_key, extent, split, -0.22, 0.18) if split else 1.0
    array = jax.random.normal(stream_key, extent, jnp.float32) * spread * level
    return jnp.minimum(jnp.maximum(array, -bound), bound).astype(dtype)


def setup_inputs(seed: int = 0) -> dict:
    splits = jax.random.split(jax.random.key(seed), 16)
    tokens = bell_draw(splits[0], (SEQS, LEN, D), 1.0, 6.0, ((0, 16), (1, 2)))
    prefix_len = touch_ends(jax.random.randint(splits[1], (SEQS,), LEN // 10, LEN // 2 + 1), jax.random.fold_in(splits[1], 1), LEN // 10, (LEN // 2 + 1) - 1).astype(jnp.int32)
    ln1_gain = jnp.clip(1.0 + 0.18 * jax.random.normal(splits[2], (D,), jnp.float32), 0.099609375, 1.8984375).astype(jnp.bfloat16)
    ln1_bias = bell_draw(splits[3], (D,), 0.3, 2.0, ((0, 8),))
    w_qkv = bell_draw(splits[4], (D, 3 * D), D ** -0.5, 0.1875, ((0, 8),))
    b_qv = bell_draw(splits[5], (2 * D,), 0.3, 2.0, ((0, 8),))
    w_out = bell_draw(splits[6], (D, D), (max(4 * D // LEN, 1)) ** -0.5, 3.0, ((0, 8),))
    b_out = bell_draw(splits[7], (D,), 0.3, 2.0, ((0, 8),))
    ln2_gain = jnp.clip(1.0 + 0.18 * jax.random.normal(splits[8], (D,), jnp.float32), 0.099609375, 1.8984375).astype(jnp.bfloat16)
    ln2_bias = bell_draw(splits[9], (D,), 0.3, 2.0, ((0, 8),))
    w_up = bell_draw(splits[10], (D, FF), D ** -0.5, 0.1875, ((0, 8),))
    b_up = bell_draw(splits[11], (FF,), 0.3, 2.0, ((0, 8),))
    w_down = bell_draw(splits[12], (FF, D), (FF // 2) ** -0.5, 0.125, ((0, 8),))
    b_down = bell_draw(splits[13], (D,), 0.3, 2.0, ((0, 8),))
    cotangent = bell_draw(splits[14], (SEQS, LEN, D), 1.0, 6.0, ((0, 16), (1, 2)))
    return {"tokens": tokens, "prefix_len": prefix_len, "ln1_gain": ln1_gain, "ln1_bias": ln1_bias, "w_qkv": w_qkv, "b_qv": b_qv, "w_out": w_out, "b_out": b_out, "ln2_gain": ln2_gain, "ln2_bias": ln2_bias, "w_up": w_up, "b_up": b_up, "w_down": w_down, "b_down": b_down, "cotangent": cotangent}


EPS = 1e-05
NEGATIVE = -1e+30

@jax.custom_vjp
def low(v):
    return lax.optimization_barrier(v.astype(jnp.bfloat16)).astype(jnp.float32)

@jax.custom_vjp
def low_back(v):
    return v

def low_keep(v):
    return (low(v), None)

def low_pass(kept, grad):
    return (grad,)

def back_keep(v):
    return (v, None)

def back_low(kept, grad):
    return (low(grad),)
low.defvjp(low_keep, low_pass)
low_back.defvjp(back_keep, back_low)

def matmul(left, right):
    return jnp.dot(left, right, precision=lax.Precision.HIGHEST)

def layer_norm(values, gain, shift):
    center = values - lax.optimization_barrier(jnp.mean(values, axis=-1, keepdims=True))
    variance = lax.optimization_barrier(jnp.mean(center * center, axis=-1, keepdims=True))
    return center * lax.rsqrt(variance + EPS) * gain + shift

def forward(params, inputs, prefix):
    gain_one, shift_one, w_qkv, b_qv, w_out, b_out, gain_two, shift_two, w_up, b_up, w_down, b_down = params
    normed = low(layer_norm(inputs, gain_one, shift_one))
    bias_row = jnp.concatenate([b_qv[:D], jnp.zeros((D,), jnp.float32), b_qv[D:]])
    project = low(low_back(matmul(normed, low(w_qkv)) + bias_row))
    queries = project[:, :D].reshape(LEN, H, HD)
    keys = project[:, D:2 * D].reshape(LEN, H, HD)
    values = project[:, 2 * D:].reshape(LEN, H, HD)
    scores = jnp.einsum('qhd,khd->hqk', queries, keys, precision=lax.Precision.HIGHEST) * HD ** (-0.5)
    scores = low_back(scores)
    places = jnp.arange(LEN)
    allowed = (places[None, :] <= places[:, None]) | (places[None, :] < prefix)
    scores = jnp.where(allowed[None], scores, NEGATIVE)
    probs = jax.nn.softmax(scores, axis=-1)
    mixed = jnp.einsum('hqk,khd->qhd', low(probs), values, precision=lax.Precision.HIGHEST).reshape(LEN, D)
    attended = low(low_back(mixed))
    branch = low_back(matmul(attended, low(w_out)) + b_out)
    middle = inputs + branch
    hidden_in = low(layer_norm(middle, gain_two, shift_two))
    pre = low_back(matmul(hidden_in, low(w_up)) + b_up)
    activated = low(jax.nn.gelu(pre, approximate=False))
    return middle + matmul(activated, low(w_down)) + b_down

def reference(tokens, prefix_len, ln1_gain, ln1_bias, w_qkv, b_qv, w_out, b_out, ln2_gain, ln2_bias, w_up, b_up, w_down, b_down, cotangent):
    params = (ln1_gain.astype(jnp.float32), ln1_bias.astype(jnp.float32), w_qkv.astype(jnp.float32), b_qv.astype(jnp.float32), w_out.astype(jnp.float32), b_out.astype(jnp.float32), ln2_gain.astype(jnp.float32), ln2_bias.astype(jnp.float32), w_up.astype(jnp.float32), b_up.astype(jnp.float32), w_down.astype(jnp.float32), b_down.astype(jnp.float32))
    zero_grads = jax.tree.map(jnp.zeros_like, params)

    def one_sequence(total, items):
        seq_tokens, seq_prefix, seq_cot = items

        def apply(weights, inputs):
            return forward(weights, inputs, seq_prefix)
        result, pull = jax.vjp(apply, params, seq_tokens.astype(jnp.float32))
        grad_params, grad_inputs = pull(seq_cot.astype(jnp.float32))
        return (jax.tree.map(jnp.add, total, grad_params), (result.astype(jnp.bfloat16), grad_inputs))
    total, (outputs, grad_inputs) = lax.scan(one_sequence, zero_grads, (tokens, prefix_len, cotangent))
    return (outputs, grad_inputs, total[0], total[1], total[2], total[3], total[4], total[5], total[6], total[7], total[8], total[9], total[10], total[11])
```

```python
import jax
import jax.numpy as jnp
from jax import lax
from jax.experimental import pallas as pl
from jax.experimental.pallas import tpu as pltpu
from jax.sharding import PartitionSpec as P

HD=64
QB=256
LOG2E=1.4426950408889634
NEG=-1e30

def dot_nn(a,b): return lax.dot_general(a,b,(((1,),(0,)),((),())),preferred_element_type=jnp.float32)
def dot_nt(a,b): return lax.dot_general(a,b,(((1,),(1,)),((),())),preferred_element_type=jnp.float32)
def dot_tn(a,b): return lax.dot_general(a,b,(((0,),(0,)),((),())),preferred_element_type=jnp.float32)

def key_extent(total, block):
    return max(total // 2, (block + 1) * QB)

def scores_t(keys, query, block, prefix, scale):
    raw = dot_nn(keys, query) * scale
    extent = raw.shape[0]
    free = block * QB
    if free:
        top, low = raw[:free], raw[free:]
    else:
        top, low = None, raw
    kpos = free + lax.broadcasted_iota(jnp.int32, low.shape, 0)
    qpos = free + lax.broadcasted_iota(jnp.int32, low.shape, 1)
    limit = jnp.maximum(qpos, prefix - 1)
    low = jnp.where(kpos <= limit, low, NEG)
    return low if top is None else jnp.concatenate([top, low], axis=0)

def fwd_kernel(info, q_ref, k_ref, v_ref, o_ref, l_ref):
    prefix = info[2]
    total = q_ref.shape[-1]
    keys = jnp.transpose(k_ref[0].astype(jnp.float32)).astype(jnp.bfloat16)
    scale = HD ** -0.5 * LOG2E
    for b in range(total // QB):
        ext = key_extent(total, b)
        sl = slice(b * QB, (b + 1) * QB)
        s = scores_t(keys[:ext], q_ref[0, :, sl], b, prefix, scale)
        top = jnp.max(s, axis=0, keepdims=True)
        p = jnp.exp2(s - top)
        denom = jnp.sum(p, axis=0, keepdims=True)
        mixed = dot_nn(v_ref[0, :, :ext], p.astype(jnp.bfloat16))
        o_ref[0, :, sl] = (mixed / denom).astype(jnp.bfloat16)
        l_ref[0, :, sl] = top + jnp.log2(denom)

def bwd_kernel(info, q_ref, k_ref, v_ref, o_ref, g_ref, l_ref, out_ref, dk_acc, dv_acc):
    prefix = info[2]
    total = q_ref.shape[-1]
    factor = HD ** -0.5
    scale = factor * LOG2E
    keep = jnp.where((info[3] > 0) & (pl.program_id(0) == 0), 0.0, 1.0).astype(jnp.float32)
    keys_t = k_ref[0]
    keys = jnp.transpose(keys_t.astype(jnp.float32)).astype(jnp.bfloat16)
    values = jnp.transpose(v_ref[0].astype(jnp.float32)).astype(jnp.bfloat16)
    dk_acc[...] = jnp.zeros_like(dk_acc)
    dv_acc[...] = jnp.zeros_like(dv_acc)
    for b in range(total // QB):
        ext = key_extent(total, b)
        sl = slice(b * QB, (b + 1) * QB)
        query = q_ref[0, :, sl]
        grad = g_ref[0, :, sl]
        delta = jnp.sum(grad.astype(jnp.float32) * o_ref[0, :, sl].astype(jnp.float32), axis=0, keepdims=True)
        s = scores_t(keys[:ext], query, b, prefix, scale)
        p = jnp.exp2(s - l_ref[0, :, sl])
        dp = dot_nn(values[:ext], grad)
        ds = (p * (dp - delta)).astype(jnp.bfloat16)
        dv_acc[:, :ext] += dot_nt(grad, p.astype(jnp.bfloat16))
        dk_acc[:, :ext] += dot_nt(query, ds)
        out_ref[info[0], 0, :, sl] = (dot_nn(keys_t[:, :ext], ds) * (factor * keep)).astype(jnp.bfloat16)
    out_ref[1, 0] = (dk_acc[...] * (factor * keep)).astype(jnp.bfloat16)
    out_ref[info[1], 0] = (dv_acc[...] * keep).astype(jnp.bfloat16)

def attend(proj, info, heads):
    total = proj.shape[-1]
    cube = proj.reshape(3 * heads, HD, total)
    blk = lambda f: pl.BlockSpec((1, HD, total), f)
    cost = pl.CostEstimate(flops=4*heads*total*total*HD, bytes_accessed=8*heads*HD*total, transcendentals=heads*total*total)
    return pl.pallas_call(
        fwd_kernel,
        out_shape=(jax.ShapeDtypeStruct((heads, HD, total), jnp.bfloat16), jax.ShapeDtypeStruct((heads, 1, total), jnp.float32)),
        grid_spec=pltpu.PrefetchScalarGridSpec(num_scalar_prefetch=1, grid=(heads,),
            in_specs=[blk(lambda h, i: (i[0]*heads+h,0,0)), blk(lambda h, i: (heads+h,0,0)), blk(lambda h, i: (i[1]*heads+h,0,0))],
            out_specs=[blk(lambda h, i: (h,0,0)), pl.BlockSpec((1,1,total), lambda h,i:(h,0,0))]),
        cost_estimate=cost, name="attend")(info, cube, cube, cube)

def attend_back(proj, info, mixed, grad, logs, heads):
    total = proj.shape[-1]
    cube = proj.reshape(3 * heads, HD, total)
    blk = lambda f: pl.BlockSpec((1, HD, total), f)
    own = lambda h, i: (h,0,0)
    cost = pl.CostEstimate(flops=10*heads*total*total*HD, bytes_accessed=16*heads*HD*total, transcendentals=heads*total*total)
    return pl.pallas_call(
        bwd_kernel,
        out_shape=jax.ShapeDtypeStruct((3, heads, HD, total), jnp.bfloat16),
        grid_spec=pltpu.PrefetchScalarGridSpec(num_scalar_prefetch=1, grid=(heads,),
            in_specs=[blk(lambda h, i: (i[0]*heads+h,0,0)), blk(lambda h, i: (heads+h,0,0)), blk(lambda h, i: (i[1]*heads+h,0,0)), blk(own), blk(own), pl.BlockSpec((1,1,total), own)],
            out_specs=pl.BlockSpec((3,1,HD,total), lambda h,i:(0,h,0,0)),
            scratch_shapes=[pltpu.VMEM((HD,total),jnp.float32)]*2),
        cost_estimate=cost, name="attend_back")(info, cube, cube, cube, mixed, grad, logs)


EPS = 1e-05
BF = jnp.bfloat16
F32 = jnp.float32


def product(left, right, left_dim, right_dim):
    return lax.dot_general(
        left, right, (((left_dim,), (right_dim,)), ((), ())), preferred_element_type=F32
    )


def moments(values):
    center = values - jnp.mean(values, axis=-1, keepdims=True)
    variance = jnp.mean(center * center, axis=-1, keepdims=True)
    inverse = lax.rsqrt(variance + EPS)
    return center * inverse, inverse


def norm_backward(grad, scaled, inverse, gain):
    inner = grad * gain
    return inverse * (
        inner
        - jnp.mean(inner, axis=-1, keepdims=True)
        - scaled * jnp.mean(inner * scaled, axis=-1, keepdims=True)
    )


class Grid:
    def __init__(self):
        self.count = lax.axis_size("fsdp")
        self.near = 1 << ((self.count.bit_length() - 1) // 2)
        self.far = self.count // self.near
        self.reps = lax.axis_size("rep")
        self.split = self.reps == 2
        place = lax.axis_index("fsdp")
        self.zi = place // self.near
        self.xi = place % self.near
        self.y = lax.axis_index("rep")
        self.c = lax.axis_index("ctx")

    def far_shift(self, array, k):
        near, far = self.near, self.far
        pairs = [(i, (i // near + k) % far * near + i % near) for i in range(self.count)]
        return lax.ppermute(array, "fsdp", pairs)

    def near_shift(self, array, k):
        near = self.near
        pairs = [(i, i // near * near + (i % near + k) % near) for i in range(self.count)]
        return lax.ppermute(array, "fsdp", pairs)

    def swap_rep(self, array):
        return lax.ppermute(array, "rep", [(0, 1), (1, 0)])

    def swap_ctx(self, array):
        return lax.ppermute(array, "ctx", [(0, 1), (1, 0)])

    def gather(self, piece):
        found = {}
        for k in range(self.far):
            line = piece if k == 0 else self.far_shift(piece, k)
            for j in range(self.near):
                found[k, j] = line if j == 0 else self.near_shift(line, j)
        return found

    def spot(self, k, j):
        return (self.zi - k) % self.far * self.near + (self.xi - j) % self.near

    def place(self, buffer, found, column, turn=0):
        for (k, j), piece in found.items():
            at = (self.spot(k, j) + turn) % self.count
            buffer = lax.dynamic_update_slice(buffer, piece[None], (at, 0, column))
        return buffer

    def scatter(self, grads):
        near, far = self.near, self.far
        cube = grads.reshape(far, near, *grads.shape[1:])
        pick = lambda k: lax.dynamic_index_in_dim(cube, (self.xi + k) % near, 1, keepdims=False)
        arrived = [self.near_shift(pick(k), k) for k in range(1, near)]

        def line(k):
            at = (self.zi + k) % far
            tail = grads.shape[1:]
            total = lax.dynamic_slice(cube, (at, self.xi, 0, 0), (1, 1, *tail)).reshape(tail).astype(F32)
            for extra in arrived:
                total += lax.dynamic_index_in_dim(extra, at, 0, keepdims=False).astype(F32)
            return total

        passed = [self.far_shift(line(k).astype(grads.dtype), k) for k in range(1, far)]
        total = line(0)
        for extra in passed:
            total += extra.astype(F32)
        return total

    def sum_rep(self, total):
        if self.split:
            low = total.astype(BF)
            return low.astype(F32) + self.swap_rep(low).astype(F32)
        return lax.psum(total, "rep")


def shards(
    tokens,
    prefix_len,
    ln1_gain,
    ln1_bias,
    w_qkv,
    b_qv,
    w_out,
    b_out,
    ln2_gain,
    ln2_bias,
    w_up,
    b_up,
    w_down,
    b_down,
    cotangent,
):
    grid = Grid()
    count, c, y = grid.count, grid.c, grid.y
    first = c == 0
    seqs, rows, width = tokens.shape
    total_len = 2 * rows
    heads_all = width // HD
    heads = (heads_all + 1) // 2
    wide = heads * HD
    skip = width - wide
    part = width // count
    ff = w_up.shape[1]
    half_ff = ff // 2
    slab = ff // count // 2
    own_tokens = tokens.reshape(rows, width)
    own_cot = cotangent.reshape(rows, width)
    lead = (y == 0) if grid.split else True

    def choose(flag, a, b):
        return a if flag is True else jnp.where(flag, a, b)

    def both(own, other):
        return jnp.where(
            first,
            jnp.concatenate([own, other], axis=0),
            jnp.concatenate([other, own], axis=0),
        )

    small = [ln1_gain, ln1_bias, b_qv, b_out, ln2_gain, ln2_bias, b_up, b_down]
    sizes = [v.shape[0] for v in small]
    vec = jnp.concatenate(small).reshape(1, -1)
    vec_full = grid.place(
        jnp.zeros((count, 1, vec.shape[1]), BF), grid.gather(vec), 0
    ).reshape(count, -1)
    small_full, at = [], 0
    for size in sizes:
        small_full.append(vec_full[:, at : at + size].astype(F32).reshape(-1))
        at += size
    gain_one, shift_one, bias_qv, bias_out, gain_two, shift_two, bias_up, bias_down = small_full

    section = lambda k: lax.dynamic_slice(w_qkv, (0, k * width + skip * c), (part, wide))
    w_q, w_k, w_v = section(0), section(1), section(2)
    if grid.split:
        sent = jnp.concatenate([jnp.where(lead, w_q, w_v), w_k], axis=1)
    else:
        sent = jnp.concatenate([w_q, w_k, w_v], axis=1)
    found = grid.gather(sent)
    full_qkv = grid.place(jnp.zeros((count, part, 3 * wide), BF), found, 0)
    if grid.split:
        other = grid.swap_rep(full_qkv[:, :, :wide])
        full_qkv = lax.dynamic_update_slice(full_qkv, other, (0, 0, 2 * wide))
    full_qkv = full_qkv.reshape(width, 3 * wide)

    up_cols = w_up.reshape(part, count, 2, slab)
    up_own = lax.dynamic_index_in_dim(up_cols, c, 2, keepdims=False).reshape(part, half_ff)
    down_own = lax.dynamic_slice(w_down, (slab * c, 0), (slab, width))
    out_own = lax.dynamic_slice(w_out, (0, skip * c), (part, wide))

    full_out = grid.place(jnp.zeros((count, part, width), BF), grid.gather(out_own), skip * c)
    half_out = lax.dynamic_slice(full_out, (0, 0, skip * c), (count, part, wide))
    full_out = lax.dynamic_update_slice(full_out, grid.swap_ctx(half_out), (0, 0, skip * (1 - c)))
    full_out = full_out.reshape(width, width)

    if grid.split:
        half_up = half_ff // 2
        turn = y * (count // 2)
        up_sent = lax.dynamic_slice(up_own, (0, half_up * y), (part, half_up))
        full_up = grid.place(jnp.zeros((count, part, half_ff), BF), grid.gather(up_sent), 0)
        other = grid.swap_rep(full_up[:, :, :half_up])
        full_up = lax.dynamic_update_slice(full_up, other, (0, 0, half_up))
    else:
        half_up, turn = half_ff, 0
        full_up = grid.place(jnp.zeros((count, part, half_ff), BF), grid.gather(up_own), 0)
    full_up = full_up.reshape(width, half_ff)
    full_down = grid.place(
        jnp.zeros((count, slab, width), BF), grid.gather(down_own), 0, turn
    ).reshape(half_ff, width)
    bias_up_own = lax.dynamic_index_in_dim(bias_up.reshape(count, 2, slab), c, 1, keepdims=False)
    if grid.split:
        bias_up_own = jnp.where(lead, bias_up_own, jnp.roll(bias_up_own, count // 2, axis=0))
    bias_up_own = bias_up_own.reshape(half_ff)

    all_tokens = both(own_tokens, grid.swap_ctx(own_tokens))
    all_cot = both(own_cot, grid.swap_ctx(own_cot))
    inputs = all_tokens.astype(F32)
    scaled_one, _ = moments(inputs)
    normed = (scaled_one * gain_one + shift_one).astype(BF)
    bias_q = lax.dynamic_slice(bias_qv, (skip * c,), (wide,))
    bias_v = lax.dynamic_slice(bias_qv, (width + skip * c,), (wide,))
    bias_row = jnp.concatenate(
        [choose(lead, bias_q, bias_v), jnp.zeros((wide,), F32), choose(lead, bias_v, bias_q)]
    )
    project = (product(full_qkv, normed, 0, 1) + bias_row[:, None]).astype(BF)
    flip = jnp.int32(0) if lead is True else jnp.where(lead, 0, 2).astype(jnp.int32)
    info = jnp.stack([flip, 2 - flip, prefix_len[0], c.astype(jnp.int32)])
    mixed, logs = attend(project, info, heads)
    own_mixed = mixed.reshape(wide, total_len)
    other_mixed = grid.swap_ctx(own_mixed)
    overlap = wide - skip
    attended = jnp.where(
        first,
        jnp.concatenate([own_mixed, other_mixed[overlap:]], axis=0),
        jnp.concatenate([other_mixed, own_mixed[overlap:]], axis=0),
    )

    middle = inputs + product(attended, full_out, 0, 0) + bias_out
    scaled_two, inverse_two = moments(middle)
    hidden_in = (scaled_two * gain_two + shift_two).astype(BF)
    pre = product(hidden_in, full_up, 1, 0) + bias_up_own
    cdf = 0.5 + 0.5 * lax.erf(pre * (0.5**0.5))
    activated = (pre * cdf).astype(BF)
    slope = (cdf + pre * jnp.exp(-0.5 * pre * pre) * (0.5 / jnp.pi) ** 0.5).astype(BF)

    own_rows = lambda array: lax.dynamic_slice(array, (rows * c, 0), (rows, array.shape[1]))
    other_rows = lambda array: lax.dynamic_slice(
        array, (rows * (1 - c), 0), (rows, array.shape[1])
    )
    partial_down = product(activated, full_down, 1, 0)
    result = own_rows(partial_down) + grid.swap_ctx(other_rows(partial_down))
    block_out = (own_rows(middle) + result + bias_down).astype(BF).reshape(seqs, rows, width)

    grad_down = product(activated, all_cot, 0, 0).astype(BF)
    grad_act = product(all_cot, full_down, 1, 1)
    grad_pre = (grad_act * slope.astype(F32)).astype(BF)
    grad_up = product(hidden_in, grad_pre, 0, 0).astype(BF)
    grad_hidden = product(grad_pre, full_up, 1, 1)
    grad_hidden = grad_hidden + grid.swap_ctx(grad_hidden)
    grad_middle = all_cot.astype(F32) + norm_backward(grad_hidden, scaled_two, inverse_two, gain_two)
    grad_branch = grad_middle.astype(BF)
    branch_cols = lax.dynamic_slice(grad_branch, (0, skip * c), (total_len, wide))
    grad_wout = product(attended, branch_cols, 1, 0).astype(BF)
    out_rows = lax.dynamic_slice(full_out, (skip * c, 0), (wide, width))
    grad_mixed = product(out_rows, grad_branch, 1, 1).astype(BF).reshape(heads, HD, total_len)
    grad_cube = attend_back(project, info, mixed, grad_mixed, logs, heads)
    grad_project = grad_cube.reshape(3 * wide, total_len)
    grad_qkv = product(normed, grad_project, 0, 1).astype(BF)
    grad_normed = product(grad_project, full_qkv, 0, 1)
    own_grad = own_rows(grad_normed) + grid.swap_ctx(other_rows(grad_normed))
    own_scaled, own_inverse = moments(own_tokens.astype(F32))
    grad_tokens = own_rows(grad_middle) + norm_backward(own_grad, own_scaled, own_inverse, gain_one)
    grad_tokens = grad_tokens.reshape(seqs, rows, width)

    own_down = grid.sum_rep(grid.scatter(
        jnp.roll(grad_down.reshape(2, -1), y, axis=0).reshape(count, slab, width)
        if grid.split
        else grad_down.reshape(count, slab, width)
    )).astype(BF)
    other_down = grid.swap_ctx(own_down)
    out_down = jnp.where(
        first,
        jnp.concatenate([own_down, other_down], axis=0),
        jnp.concatenate([other_down, own_down], axis=0),
    ).astype(F32)

    up_cube = grad_up.reshape(count, part, half_ff)
    if grid.split:
        mine = up_cube[:, :, :half_up].astype(F32) + grid.swap_rep(up_cube[:, :, half_up:]).astype(F32)
        mine = grid.scatter(mine.astype(BF)).astype(BF)
        other = grid.swap_rep(mine)
        own_up = jnp.where(
            lead,
            jnp.concatenate([mine, other], axis=1),
            jnp.concatenate([other, mine], axis=1),
        )
    else:
        own_up = grid.sum_rep(grid.scatter(up_cube)).astype(BF)
    other_up = grid.swap_ctx(own_up)
    pair = lambda a, b: jnp.stack(
        [a.reshape(part, count, slab), b.reshape(part, count, slab)], axis=2
    ).reshape(part, ff)
    out_up = jnp.where(first, pair(own_up, other_up), pair(other_up, own_up)).astype(F32)

    own_wout = grid.sum_rep(grid.scatter(grad_wout.reshape(count, part, wide))).astype(BF)
    other_wout = grid.swap_ctx(own_wout)
    out_wout = jnp.where(
        first,
        jnp.concatenate([own_wout, other_wout[:, overlap:]], axis=1),
        jnp.concatenate([other_wout, own_wout[:, overlap:]], axis=1),
    ).astype(F32)

    qkv_cube = grad_qkv.reshape(count, part, 3 * wide)
    if grid.split:
        arrived = grid.swap_rep(qkv_cube[:, :, 2 * wide :])
        mine = qkv_cube[:, :, :wide].astype(F32) + arrived.astype(F32)
        mine = jnp.concatenate([mine.astype(BF), qkv_cube[:, :, wide : 2 * wide]], axis=2)
        mine = grid.scatter(mine).astype(BF)
        other = grid.swap_rep(mine)
        centre = (mine[:, wide:].astype(F32) + other[:, wide:].astype(F32)).astype(BF)
        own_sections = [
            jnp.where(lead, mine[:, :wide], other[:, :wide]),
            centre,
            jnp.where(lead, other[:, :wide], mine[:, :wide]),
        ]
        own_qkv = jnp.concatenate(own_sections, axis=1)
    else:
        own_qkv = grid.sum_rep(grid.scatter(qkv_cube)).astype(BF)
    other_qkv = grid.swap_ctx(own_qkv)
    low_qkv = jnp.where(first, own_qkv, other_qkv)
    high_qkv = jnp.where(first, other_qkv, own_qkv)
    pieces = []
    for k in range(3):
        pieces.append(low_qkv[:, k * wide : (k + 1) * wide])
        pieces.append(high_qkv[:, k * wide + overlap : (k + 1) * wide])
    out_qkv = jnp.concatenate(pieces, axis=1).astype(F32)

    once = jnp.where(first, 1.0, 0.0).astype(F32)
    spread = lambda values, start, size: lax.dynamic_update_slice(
        jnp.zeros((size,), F32), values, (start,)
    )
    project_sums = jnp.sum(grad_cube.astype(F32), axis=3).reshape(3, wide)
    sums_q = choose(lead, project_sums[0], project_sums[2])
    sums_v = choose(lead, project_sums[2], project_sums[0])
    grad_bias_qv = jnp.concatenate(
        [spread(sums_q, skip * c, width), spread(sums_v, skip * c, width)]
    )
    pre_sums = jnp.sum(grad_pre.astype(F32), axis=0).reshape(count, slab)
    if grid.split:
        pre_sums = jnp.where(lead, pre_sums, jnp.roll(pre_sums, count // 2, axis=0))
    grad_bias_up = lax.dynamic_update_slice(
        jnp.zeros((count, 2, slab), F32), pre_sums[:, None], (0, c, 0)
    )
    vectors = [
        jnp.sum(own_grad * own_scaled, axis=0),
        jnp.sum(own_grad, axis=0),
        grad_bias_qv,
        once * jnp.sum(grad_branch.astype(F32), axis=0),
        once * jnp.sum(grad_hidden * scaled_two, axis=0),
        once * jnp.sum(grad_hidden, axis=0),
        grad_bias_up,
        once * jnp.sum(all_cot.astype(F32), axis=0),
    ]
    table = jnp.concatenate([v.reshape(count, -1) for v in vectors], axis=1)
    table = table + grid.swap_ctx(table)
    table = table + grid.swap_rep(table) if grid.split else lax.psum(table, "rep")
    summed = grid.scatter(table[:, None, :]).reshape(-1)
    outs, at = [], 0
    for size in sizes:
        outs.append(summed[at : at + size])
        at += size
    return (
        block_out,
        grad_tokens,
        outs[0],
        outs[1],
        out_qkv,
        outs[2],
        out_wout,
        outs[3],
        outs[4],
        outs[5],
        out_up,
        outs[6],
        out_down,
        outs[7],
    )


def solution(mesh):
    placed = (
        P(("fsdp", "rep"), "ctx", None),
        P(("fsdp", "rep")),
        P("fsdp"),
        P("fsdp"),
        P("fsdp", None),
        P("fsdp"),
        P("fsdp", None),
        P("fsdp"),
        P("fsdp"),
        P("fsdp"),
        P("fsdp", None),
        P("fsdp"),
        P("fsdp", None),
        P("fsdp"),
        P(("fsdp", "rep"), "ctx", None),
    )
    return jax.shard_map(
        shards,
        mesh=mesh,
        in_specs=placed,
        out_specs=(
            P(("fsdp", "rep"), "ctx", None),
            P(("fsdp", "rep"), "ctx", None),
            P("fsdp"),
            P("fsdp"),
            P("fsdp", None),
            P("fsdp"),
            P("fsdp", None),
            P("fsdp"),
            P("fsdp"),
            P("fsdp"),
            P("fsdp", None),
            P("fsdp"),
            P("fsdp", None),
            P("fsdp"),
        ),
        check_vma=False,
    )
```

```python
import jax
import jax.numpy as jnp
from jax import lax
from jax.experimental import pallas as pl
from jax.experimental.pallas import tpu as pltpu
from jax.sharding import PartitionSpec as P

HD=64
QB=256
LOG2E=1.4426950408889634
NEG=-1e30

def dot_nn(a,b): return lax.dot_general(a,b,(((1,),(0,)),((),())),preferred_element_type=jnp.float32)
def dot_nt(a,b): return lax.dot_general(a,b,(((1,),(1,)),((),())),preferred_element_type=jnp.float32)
def dot_tn(a,b): return lax.dot_general(a,b,(((0,),(0,)),((),())),preferred_element_type=jnp.float32)

def key_extent(total, block):
    return max(total // 2, (block + 1) * QB)

def scores_t(keys, query, block, prefix, scale):
    raw = dot_nn(keys, query) * scale
    extent = raw.shape[0]
    free = block * QB
    if free:
        top, low = raw[:free], raw[free:]
    else:
        top, low = None, raw
    kpos = free + lax.broadcasted_iota(jnp.int32, low.shape, 0)
    qpos = free + lax.broadcasted_iota(jnp.int32, low.shape, 1)
    limit = jnp.maximum(qpos, prefix - 1)
    low = jnp.where(kpos <= limit, low, NEG)
    return low if top is None else jnp.concatenate([top, low], axis=0)

def fwd_kernel(info, q_ref, k_ref, v_ref, o_ref, l_ref):
    prefix = info[2]
    total = q_ref.shape[-1]
    keys = jnp.transpose(k_ref[0].astype(jnp.float32)).astype(jnp.bfloat16)
    scale = HD ** -0.5 * LOG2E
    for b in range(total // QB):
        ext = key_extent(total, b)
        sl = slice(b * QB, (b + 1) * QB)
        s = scores_t(keys[:ext], q_ref[0, :, sl], b, prefix, scale)
        top = jnp.max(s, axis=0, keepdims=True)
        p = jnp.exp2(s - top)
        denom = jnp.sum(p, axis=0, keepdims=True)
        mixed = dot_nn(v_ref[0, :, :ext], p.astype(jnp.bfloat16))
        o_ref[0, :, sl] = (mixed / denom).astype(jnp.bfloat16)
        l_ref[0, :, sl] = top + jnp.log2(denom)

def bwd_kernel(info, q_ref, k_ref, v_ref, o_ref, g_ref, l_ref, out_ref, dk_acc, dv_acc):
    prefix = info[2]
    total = q_ref.shape[-1]
    factor = HD ** -0.5
    scale = factor * LOG2E
    keep = jnp.where((info[3] == 0) & (pl.program_id(0) == pl.num_programs(0) - 1), 0.0, 1.0).astype(jnp.float32)
    keys_t = k_ref[0]
    keys = jnp.transpose(keys_t.astype(jnp.float32)).astype(jnp.bfloat16)
    values = jnp.transpose(v_ref[0].astype(jnp.float32)).astype(jnp.bfloat16)
    dk_acc[...] = jnp.zeros_like(dk_acc)
    dv_acc[...] = jnp.zeros_like(dv_acc)
    for b in range(total // QB):
        ext = key_extent(total, b)
        sl = slice(b * QB, (b + 1) * QB)
        query = q_ref[0, :, sl]
        grad = g_ref[0, :, sl]
        delta = jnp.sum(grad.astype(jnp.float32) * o_ref[0, :, sl].astype(jnp.float32), axis=0, keepdims=True)
        s = scores_t(keys[:ext], query, b, prefix, scale)
        p = jnp.exp2(s - l_ref[0, :, sl])
        dp = dot_nn(values[:ext], grad)
        ds = (p * (dp - delta)).astype(jnp.bfloat16)
        dv_acc[:, :ext] += dot_nt(grad, p.astype(jnp.bfloat16))
        dk_acc[:, :ext] += dot_nt(query, ds)
        out_ref[info[0], 0, :, sl] = (dot_nn(keys_t[:, :ext], ds) * (factor * keep)).astype(jnp.bfloat16)
    out_ref[1, 0] = (dk_acc[...] * (factor * keep)).astype(jnp.bfloat16)
    out_ref[info[1], 0] = (dv_acc[...] * keep).astype(jnp.bfloat16)

def attend(proj, info, heads):
    total = proj.shape[-1]
    cube = proj.reshape(3 * heads, HD, total)
    blk = lambda f: pl.BlockSpec((1, HD, total), f)
    cost = pl.CostEstimate(flops=4*heads*total*total*HD, bytes_accessed=8*heads*HD*total, transcendentals=heads*total*total)
    return pl.pallas_call(
        fwd_kernel,
        out_shape=(jax.ShapeDtypeStruct((heads, HD, total), jnp.bfloat16), jax.ShapeDtypeStruct((heads, 1, total), jnp.float32)),
        grid_spec=pltpu.PrefetchScalarGridSpec(num_scalar_prefetch=1, grid=(heads,),
            in_specs=[blk(lambda h, i: (i[0]*heads+h,0,0)), blk(lambda h, i: (heads+h,0,0)), blk(lambda h, i: (i[1]*heads+h,0,0))],
            out_specs=[blk(lambda h, i: (h,0,0)), pl.BlockSpec((1,1,total), lambda h,i:(h,0,0))]),
        cost_estimate=cost, name="attend")(info, cube, cube, cube)

def attend_back(proj, info, mixed, grad, logs, heads):
    total = proj.shape[-1]
    cube = proj.reshape(3 * heads, HD, total)
    blk = lambda f: pl.BlockSpec((1, HD, total), f)
    own = lambda h, i: (h,0,0)
    cost = pl.CostEstimate(flops=10*heads*total*total*HD, bytes_accessed=16*heads*HD*total, transcendentals=heads*total*total)
    return pl.pallas_call(
        bwd_kernel,
        out_shape=jax.ShapeDtypeStruct((3, heads, HD, total), jnp.bfloat16),
        grid_spec=pltpu.PrefetchScalarGridSpec(num_scalar_prefetch=1, grid=(heads,),
            in_specs=[blk(lambda h, i: (i[0]*heads+h,0,0)), blk(lambda h, i: (heads+h,0,0)), blk(lambda h, i: (i[1]*heads+h,0,0)), blk(own), blk(own), pl.BlockSpec((1,1,total), own)],
            out_specs=pl.BlockSpec((3,1,HD,total), lambda h,i:(0,h,0,0)),
            scratch_shapes=[pltpu.VMEM((HD,total),jnp.float32)]*2),
        cost_estimate=cost, name="attend_back")(info, cube, cube, cube, mixed, grad, logs)


EPS = 1e-05
BF = jnp.bfloat16
F32 = jnp.float32


def product(left, right, left_dim, right_dim):
    return lax.dot_general(
        left, right, (((left_dim,), (right_dim,)), ((), ())), preferred_element_type=F32
    )


def moments(values):
    center = values - jnp.mean(values, axis=-1, keepdims=True)
    variance = jnp.mean(center * center, axis=-1, keepdims=True)
    inverse = lax.rsqrt(variance + EPS)
    return center * inverse, inverse


def norm_backward(grad, scaled, inverse, gain):
    inner = grad * gain
    return inverse * (
        inner
        - jnp.mean(inner, axis=-1, keepdims=True)
        - scaled * jnp.mean(inner * scaled, axis=-1, keepdims=True)
    )


def hold(values, *after):
    return lax.optimization_barrier((values, after))[0]


def assemble(info, arrays, jobs, shape):
    total, rows = len(arrays), shape[1]

    def kernel(info_ref, *refs):
        out, sems = refs[total], refs[total + 1]

        def span(column, size):
            if isinstance(column, tuple):
                return pl.ds(pl.multiple_of(info_ref[column[0]], 128), size)
            return slice(column, column + size)

        copies = [
            pltpu.make_async_copy(
                refs[place].at[(*lead, slice(0, rows), span(source, size))],
                out.at[info_ref[block], :, span(target, size)],
                sems.at[i],
            )
            for i, (place, lead, block, source, target, size) in enumerate(jobs)
        ]
        for copy in copies:
            copy.start()
        for copy in copies:
            copy.wait()

    anywhere = pl.BlockSpec(memory_space=pl.ANY)
    return pl.pallas_call(
        kernel,
        out_shape=jax.ShapeDtypeStruct(shape, arrays[0].dtype),
        grid_spec=pltpu.PrefetchScalarGridSpec(
            num_scalar_prefetch=1,
            grid=(1,),
            in_specs=[anywhere] * total,
            out_specs=pl.BlockSpec(shape, lambda i, s: (0, 0, 0)),
            scratch_shapes=[pltpu.SemaphoreType.DMA((len(jobs),))],
        ),
        cost_estimate=pl.CostEstimate(
            flops=0, bytes_accessed=4 * shape[0] * shape[1] * shape[2], transcendentals=0
        ),
        name="assemble",
    )(info, *arrays)


class Grid:
    def __init__(self):
        self.count = lax.axis_size("fsdp")
        self.near = 1 << ((self.count.bit_length() - 1) // 2)
        self.far = self.count // self.near
        self.reps = lax.axis_size("rep")
        self.split = self.reps == 2 and self.near == 2
        place = lax.axis_index("fsdp")
        self.zi = place // self.near
        self.xi = place % self.near
        self.y = lax.axis_index("rep")
        self.c = lax.axis_index("ctx")
        order = [k for pair in zip(range(1, self.far), range(self.far - 1, 0, -1)) for k in pair]
        self.steps = list(dict.fromkeys(order))

    def far_shift(self, array, k):
        near, far = self.near, self.far
        pairs = [(i, (i // near + k) % far * near + i % near) for i in range(self.count)]
        return lax.ppermute(array, "fsdp", pairs)

    def near_shift(self, array, k):
        near = self.near
        pairs = [(i, i // near * near + (i % near + k) % near) for i in range(self.count)]
        return lax.ppermute(array, "fsdp", pairs)

    def swap_rep(self, array):
        return lax.ppermute(array, "rep", [(0, 1), (1, 0)])

    def swap_ctx(self, array):
        return lax.ppermute(array, "ctx", [(0, 1), (1, 0)])

    def lines(self, piece):
        return [piece] + [self.far_shift(piece, k) for k in range(1, self.far)]

    def spots(self):
        return [
            (self.zi - k) % self.far * self.near + (self.xi - j) % self.near
            for j in range(self.near)
            for k in range(self.far)
        ]

    def gather_all(self, piece):
        return lax.all_gather(piece, "fsdp", axis=0, tiled=True)

    def scatter_all(self, grads):
        return lax.psum_scatter(grads, "fsdp", scatter_dimension=0, tiled=True)

    def groups(self):
        steps = sorted(range(1, self.far), key=lambda k: (abs(2 * k - self.far), k)) + [0]
        return steps[: self.far // 2], steps[self.far // 2 :]

    def pick_lines(self, cube, steps):
        return jnp.stack(
            [
                lax.dynamic_index_in_dim(cube, (self.zi + k) % self.far, 0, keepdims=False)
                for k in steps
            ]
        )

    def near_send(self, cube):
        return self.near_shift(
            lax.dynamic_index_in_dim(cube, (self.xi + 1) % self.near, 1, keepdims=False), 1
        )

    def line_sum(self, cube, arrived, at):
        tail = cube.shape[2:]
        own = lax.dynamic_slice(cube, (at, self.xi, 0, 0), (1, 1, *tail)).reshape(tail)
        other = lax.dynamic_index_in_dim(arrived, at, 0, keepdims=False)
        return own.astype(F32) + other.astype(F32)

    def near_sum(self, cube, arrived, k):
        return self.line_sum(cube, arrived, (self.zi + k) % self.far)

    def scatter(self, grads):
        cube = grads.reshape(self.far, self.near, *grads.shape[1:])
        arrived = self.near_send(cube)
        passed = [
            self.far_shift(self.near_sum(cube, arrived, k).astype(grads.dtype), k)
            for k in range(1, self.far)
        ]
        total = self.near_sum(cube, arrived, 0)
        for extra in passed:
            total += extra.astype(F32)
        return total

    def sum_rep(self, total):
        if self.split:
            return total.astype(F32) + self.swap_rep(total.astype(BF)).astype(F32)
        return lax.psum(total.astype(F32), "rep")


def shards(
    tokens,
    prefix_len,
    ln1_gain,
    ln1_bias,
    w_qkv,
    b_qv,
    w_out,
    b_out,
    ln2_gain,
    ln2_bias,
    w_up,
    b_up,
    w_down,
    b_down,
    cotangent,
):
    grid = Grid()
    count, c, y = grid.count, grid.c, grid.y
    first = c == 0
    seqs, rows, width = tokens.shape
    total_len = 2 * rows
    heads_all = width // HD
    heads = (heads_all + 1) // 2
    wide = heads * HD
    skip = width - wide
    part = width // count
    ff = w_up.shape[1]
    half_ff = ff // 2
    slab = ff // count // 2
    own_tokens = tokens.reshape(rows, width)
    own_cot = cotangent.reshape(rows, width)
    lead = (y == 0) if grid.split else True

    def choose(flag, a, b):
        return a if flag is True else jnp.where(flag, a, b)

    def both(own, other):
        return jnp.where(
            first,
            jnp.concatenate([own, other], axis=0),
            jnp.concatenate([other, own], axis=0),
        )

    small = [ln1_gain, ln1_bias, b_qv, b_out, ln2_gain, ln2_bias, b_up, b_down]
    sizes = [v.shape[0] for v in small]
    vec = jnp.concatenate(small)

    def section(k):
        low = w_qkv[:, k * width : k * width + wide]
        return jnp.where(first, low, w_qkv[:, k * width + skip : k * width + skip + wide])

    w_q, w_k, w_v = section(0), section(1), section(2)
    down_own = lax.dynamic_slice(w_down, (slab * c, 0), (slab, width))
    out_own = lax.dynamic_slice(w_out, (0, skip * c), (part, wide))
    up_cols = w_up.reshape(part, count, 2, slab)
    up_own = lax.dynamic_index_in_dim(up_cols, c, 2, keepdims=False).reshape(part, half_ff)
    up_skip = half_ff // 2 // 128 * 128
    up_wide = half_ff - up_skip
    if grid.split:
        far = grid.far
        mine = jnp.where(lead, w_q, w_v)
        tail_rows = -(-vec.shape[0] // (2 * wide))
        tail = jnp.pad(vec, (0, 8 * 2 * wide - vec.shape[0])).reshape(8, 2 * wide)
        lines = grid.lines(
            jnp.concatenate([jnp.concatenate([mine, w_k], axis=1), tail], axis=0)
        )
        up_cut = lambda rep: lax.dynamic_slice(up_own, (0, up_skip * rep), (part, up_wide))
        lines, up_mine, out_own, down_own = hold((lines, up_cut(y), out_own, down_own))
        half_out = grid.gather_all(out_own)
        full_down = grid.gather_all(down_own)
        qkv_near = jnp.stack(lines)
        qkv_next = grid.near_shift(qkv_near, 1)
        up_lines = grid.lines(up_mine)
        qkv_near, qkv_next, up_lines = hold((qkv_near, qkv_next, up_lines))
        qkv_other = grid.swap_rep(
            jnp.stack([qkv_near[:, :part, :wide], qkv_next[:, :part, :wide]])
        )
        up_near = jnp.stack(up_lines)
        up_next = grid.near_shift(up_near, 1)
        qkv_near, qkv_next, qkv_other, up_near, up_next = hold(
            (qkv_near, qkv_next, qkv_other, up_near, up_next)
        )
        spots = jnp.stack(
            grid.spots() + [up_skip * y, (up_wide - up_skip) * (1 - y), up_wide * (1 - y)]
        ).astype(jnp.int32)
        full_qkv = assemble(
            spots,
            [qkv_near, qkv_next, qkv_other],
            [(i // far, (i % far,), i, 0, 0, 2 * wide) for i in range(count)]
            + [(2, (i // far, i % far), i, 0, 2 * wide, wide) for i in range(count)],
            (count, part, 3 * wide),
        )
        tails = jnp.concatenate([qkv_near, qkv_next])[:, part : part + tail_rows]
        chosen = spots[None, :count, None] == jnp.arange(count)[:, None, None]
        vec_full = jnp.sum(
            jnp.where(chosen, tails.reshape(1, count, -1).astype(F32), 0.0), axis=1
        )
        up_other = grid.swap_rep(jnp.stack([up_near, up_next]))
    else:
        full_qkv = grid.gather_all(jnp.concatenate([w_q, w_k, w_v], axis=1))
        vec_full = grid.gather_all(vec.reshape(1, -1)).astype(F32)
        half_out = grid.gather_all(out_own)
        full_up = grid.gather_all(up_own)
        full_down = grid.gather_all(down_own)
    full_qkv = full_qkv.reshape(width, 3 * wide)
    small_full, at = [], 0
    for size in sizes:
        small_full.append(vec_full[:, at : at + size].reshape(-1))
        at += size
    gain_one, shift_one, bias_qv, bias_out, gain_two, shift_two, bias_up, bias_down = small_full

    all_tokens = both(own_tokens, grid.swap_ctx(own_tokens))
    all_cot = both(own_cot, grid.swap_ctx(own_cot))
    inputs = all_tokens.astype(F32)
    scaled_one, _ = moments(inputs)
    normed = (scaled_one * gain_one + shift_one).astype(BF)
    bias_q = lax.dynamic_slice(bias_qv, (skip * c,), (wide,))
    bias_v = lax.dynamic_slice(bias_qv, (width + skip * c,), (wide,))
    bias_row = jnp.concatenate(
        [choose(lead, bias_q, bias_v), jnp.zeros((wide,), F32), choose(lead, bias_v, bias_q)]
    )
    project = (product(full_qkv, normed, 0, 1) + bias_row[:, None]).astype(BF)
    flip = jnp.int32(0) if lead is True else jnp.where(lead, 0, 2).astype(jnp.int32)
    info = jnp.stack([flip, 2 - flip, prefix_len[0], c.astype(jnp.int32)])
    mixed, logs = attend(project, info, heads)
    other_out = grid.swap_ctx(half_out)
    full_out = jnp.concatenate(
        [jnp.where(first, half_out, other_out)[:, :skip], jnp.where(first, other_out, half_out)],
        axis=1,
    )
    bias_up_own = lax.dynamic_index_in_dim(bias_up.reshape(count, 2, slab), c, 1, keepdims=False)
    bias_up_own = bias_up_own.reshape(half_ff)
    own_mixed = mixed.reshape(wide, total_len)
    other_mixed = grid.swap_ctx(own_mixed)
    overlap = wide - skip
    attended = jnp.where(
        first,
        jnp.concatenate([own_mixed, other_mixed[overlap:]], axis=0),
        jnp.concatenate([other_mixed, own_mixed[overlap:]], axis=0),
    )

    middle = inputs + product(attended, full_out, 0, 0) + bias_out
    if grid.split:
        middle, up_other = hold((middle, up_other))
        full_up = assemble(
            spots,
            [up_near, up_next, up_other],
            [(i // far, (i % far,), i, 0, (count,), up_wide) for i in range(count)]
            + [
                (2, (i // far, i % far), i, (count + 1,), (count + 2,), up_skip)
                for i in range(count)
            ],
            (count, part, half_ff),
        ).reshape(width, half_ff)
    scaled_two, inverse_two = moments(middle)
    hidden_in = (scaled_two * gain_two + shift_two).astype(BF)
    pre = product(hidden_in, full_up, 1, 0) + bias_up_own
    cdf = 0.5 + 0.5 * lax.erf(pre * (0.5**0.5))
    activated = (pre * cdf).astype(BF)
    slope = (cdf + pre * jnp.exp(-0.5 * pre * pre) * (0.5 / jnp.pi) ** 0.5).astype(BF)

    own_rows = lambda array: lax.dynamic_slice(array, (rows * c, 0), (rows, array.shape[1]))
    other_rows = lambda array: lax.dynamic_slice(
        array, (rows * (1 - c), 0), (rows, array.shape[1])
    )

    grad_down = product(activated, all_cot, 0, 0).astype(BF)
    full_down, grad_down = hold((full_down, grad_down))
    grad_act = product(all_cot, full_down, 1, 1)
    grad_pre = (grad_act * slope.astype(F32)).astype(BF)
    if grid.split:
        own_down = grid.scatter_all(grad_down)
        grad_cut = lambda rep: lax.dynamic_slice(grad_pre, (0, up_skip * rep), (total_len, up_wide))
        up_sent = product(hidden_in, grad_cut(1 - y), 0, 0).astype(BF)
        up_mine = product(hidden_in, grad_cut(y), 0, 0).astype(BF)
        rows_cube = lambda g: g.reshape(far, grid.near, part, g.shape[1])
        groups = grid.groups()
        up_sent, up_mine = rows_cube(up_sent), rows_cube(up_mine)
        up_sent = [grid.swap_rep(grid.pick_lines(up_sent, steps)) for steps in groups]
    else:
        own_down = grid.scatter_all(grad_down)
        grad_up = product(hidden_in, grad_pre, 0, 0).astype(BF)
    grad_hidden = product(grad_pre, full_up, 1, 1)
    if grid.split:
        grad_hidden, up_mine, up_sent[0], activated = hold(
            (grad_hidden, up_mine, up_sent[0], activated)
        )
        merge = lambda i: (
            grid.pick_lines(up_mine, groups[i]).astype(F32) + up_sent[i].astype(F32)
        ).astype(BF)
        up_cubes = [merge(0)]
        up_near = [grid.near_send(up_cubes[0])]
    partial_down = product(activated, full_down, 1, 0)
    result = own_rows(partial_down) + grid.swap_ctx(other_rows(partial_down))
    block_out = (own_rows(middle) + result + bias_down).astype(BF).reshape(seqs, rows, width)
    grad_hidden = grad_hidden + grid.swap_ctx(grad_hidden)
    grad_middle = all_cot.astype(F32) + norm_backward(grad_hidden, scaled_two, inverse_two, gain_two)
    grad_branch = grad_middle.astype(BF)
    if grid.split:
        grad_branch, up_near, up_cubes, block_out = hold(
            (grad_branch, up_near, up_cubes, block_out)
        )
        send_far = lambda i: {
            k: grid.far_shift(grid.line_sum(up_cubes[i], up_near[i], at).astype(BF), k)
            for at, k in enumerate(groups[i])
            if k
        }
        up_far = send_far(0)
    branch_cols = lax.dynamic_slice(grad_branch, (0, skip * c), (total_len, wide))
    grad_wout = product(attended, branch_cols, 1, 0).astype(BF)
    out_rows = lax.dynamic_slice(full_out, (skip * c, 0), (wide, width))
    grad_mixed = product(out_rows, grad_branch, 1, 1).astype(BF).reshape(heads, HD, total_len)
    if grid.split:
        up_sent[1], grad_wout, grad_mixed = hold((up_sent[1], grad_wout, grad_mixed))
        up_cubes.append(merge(1))
        up_near.append(grid.near_send(up_cubes[1]))
        out_cube = rows_cube(grad_wout)
        out_near = grid.near_send(out_cube)
    grad_cube = attend_back(project, info, mixed, grad_mixed, logs, heads)
    if grid.split:
        grad_cube, up_near, up_cubes, up_far, out_near, out_cube = hold(
            (grad_cube, up_near, up_cubes, up_far, out_near, out_cube)
        )
        up_far.update(send_far(1))
        out_far = [
            grid.far_shift(grid.near_sum(out_cube, out_near, k).astype(BF), k)
            for k in range(1, far)
        ]
    grad_project = grad_cube.reshape(3 * wide, total_len)
    qkv_sent = product(normed, grad_project[2 * wide :], 0, 1).astype(BF)
    qkv_mine = product(normed, grad_project[: 2 * wide], 0, 1).astype(BF)
    if grid.split:
        qkv_sent, qkv_mine, grad_project = hold((qkv_sent, qkv_mine, grad_project))
        qkv_sent = grid.swap_rep(qkv_sent)
        key_cube = rows_cube(qkv_mine[:, wide:])
        key_near = grid.near_send(key_cube)
    grad_normed = product(grad_project, full_qkv, 0, 1)
    own_grad = own_rows(grad_normed) + grid.swap_ctx(other_rows(grad_normed))
    own_scaled, own_inverse = moments(own_tokens.astype(F32))
    grad_tokens = own_rows(grad_middle) + norm_backward(own_grad, own_scaled, own_inverse, gain_one)
    grad_tokens = grad_tokens.reshape(seqs, rows, width)

    if grid.split:
        qkv_sent, qkv_mine, key_near, key_cube, up_far, out_far, own_grad = hold(
            (qkv_sent, qkv_mine, key_near, key_cube, up_far, out_far, own_grad)
        )
        low = qkv_mine[:, :wide].astype(F32) + qkv_sent.astype(F32)
        low_cube = rows_cube(low.astype(BF))
        low_near = grid.near_send(low_cube)
        key_far = [
            grid.far_shift(grid.near_sum(key_cube, key_near, k).astype(BF), k)
            for k in range(1, far)
        ]
        up_total = grid.line_sum(up_cubes[1], up_near[1], far - far // 2 - 1)
        for extra in up_far.values():
            up_total += extra.astype(F32)
        out_total = grid.near_sum(out_cube, out_near, 0)
        for extra in out_far:
            out_total += extra.astype(F32)
        pair = jnp.concatenate([up_total.astype(BF), out_total.astype(BF)], axis=1)
        pair_other = grid.swap_rep(pair)
        low_near, low_cube, pair, pair_other, key_far = hold(
            (low_near, low_cube, pair, pair_other, key_far)
        )
        low_far = [
            grid.far_shift(grid.near_sum(low_cube, low_near, k).astype(BF), k)
            for k in range(1, far)
        ]
    own_down = grid.sum_rep(own_down).astype(BF)
    other_down = grid.swap_ctx(own_down)
    out_down = jnp.where(
        first,
        jnp.concatenate([own_down, other_down], axis=0),
        jnp.concatenate([other_down, own_down], axis=0),
    ).astype(F32)

    if grid.split:
        mine, other = pair[:, :up_wide], pair_other[:, :up_wide]
        own_up = jnp.concatenate(
            [jnp.where(lead, mine, other)[:, :up_skip], jnp.where(lead, other, mine)], axis=1
        )
    else:
        own_up = grid.sum_rep(grid.scatter_all(grad_up)).astype(BF)
    other_up = grid.swap_ctx(own_up)
    weave = lambda a, b: jnp.stack(
        [a.reshape(part, count, slab), b.reshape(part, count, slab)], axis=2
    ).reshape(part, ff)
    out_up = weave(
        jnp.where(first, own_up, other_up), jnp.where(first, other_up, own_up)
    ).astype(F32)

    if grid.split:
        own_wout = (pair[:, up_wide:].astype(F32) + pair_other[:, up_wide:].astype(F32)).astype(BF)
    else:
        own_wout = grid.sum_rep(grid.scatter_all(grad_wout)).astype(BF)
    other_wout = grid.swap_ctx(own_wout)
    out_wout = jnp.concatenate(
        [jnp.where(first, own_wout, other_wout)[:, :skip], jnp.where(first, other_wout, own_wout)],
        axis=1,
    ).astype(F32)

    if grid.split:
        keys = grid.near_sum(key_cube, key_near, 0)
        for extra in key_far:
            keys += extra.astype(F32)
        centre = grid.sum_rep(keys).astype(BF)
        low_far, out_up, out_wout, out_down, centre = hold(
            (low_far, out_up, out_wout, out_down, centre)
        )
        mine = grid.near_sum(low_cube, low_near, 0)
        for extra in low_far:
            mine += extra.astype(F32)
        mine = mine.astype(BF)
        other = grid.swap_rep(mine)
        own_sections = [
            jnp.where(lead, mine, other),
            centre,
            jnp.where(lead, other, mine),
        ]
    else:
        own_qkv = [grid.sum_rep(grid.scatter_all(g)).astype(BF) for g in (qkv_mine, qkv_sent)]
        own_sections = [own_qkv[0][:, :wide], own_qkv[0][:, wide:], own_qkv[1]]
    own_qkv = jnp.concatenate(own_sections, axis=1)
    other_qkv = grid.swap_ctx(own_qkv)
    low_qkv = jnp.where(first, own_qkv, other_qkv)
    high_qkv = jnp.where(first, other_qkv, own_qkv)
    pieces = []
    for k in range(3):
        pieces.append(low_qkv[:, k * wide : k * wide + skip])
        pieces.append(high_qkv[:, k * wide : (k + 1) * wide])
    out_qkv = jnp.concatenate(pieces, axis=1).astype(F32)

    once = jnp.where(first, 1.0, 0.0).astype(F32)
    spread = lambda values, start, size: lax.dynamic_update_slice(
        jnp.zeros((size,), F32), values, (start,)
    )
    project_sums = jnp.sum(grad_cube.astype(F32), axis=3).reshape(3, wide)
    sums_q = choose(lead, project_sums[0], project_sums[2])
    sums_v = choose(lead, project_sums[2], project_sums[0])
    grad_bias_qv = jnp.concatenate(
        [spread(sums_q, skip * c, width), spread(sums_v, skip * c, width)]
    )
    pre_sums = jnp.sum(grad_pre.astype(F32), axis=0).reshape(count, slab)
    grad_bias_up = lax.dynamic_update_slice(
        jnp.zeros((count, 2, slab), F32), pre_sums[:, None], (0, c, 0)
    )
    vectors = [
        jnp.sum(own_grad * own_scaled, axis=0),
        jnp.sum(own_grad, axis=0),
        grad_bias_qv,
        once * jnp.sum(grad_branch.astype(F32), axis=0),
        once * jnp.sum(grad_hidden * scaled_two, axis=0),
        once * jnp.sum(grad_hidden, axis=0),
        grad_bias_up,
        once * jnp.sum(all_cot.astype(F32), axis=0),
    ]
    table = jnp.concatenate([v.reshape(count, -1) for v in vectors], axis=1)
    table = table + grid.swap_ctx(table)
    table = table + grid.swap_rep(table) if grid.split else lax.psum(table, "rep")
    summed = grid.scatter(table[:, None, :]).reshape(-1)
    outs, at = [], 0
    for size in sizes:
        outs.append(summed[at : at + size])
        at += size
    return (
        block_out,
        grad_tokens,
        outs[0],
        outs[1],
        out_qkv,
        outs[2],
        out_wout,
        outs[3],
        outs[4],
        outs[5],
        out_up,
        outs[6],
        out_down,
        outs[7],
    )


def solution(mesh):
    placed = (
        P(("fsdp", "rep"), "ctx", None),
        P(("fsdp", "rep")),
        P("fsdp"),
        P("fsdp"),
        P("fsdp", None),
        P("fsdp"),
        P("fsdp", None),
        P("fsdp"),
        P("fsdp"),
        P("fsdp"),
        P("fsdp", None),
        P("fsdp"),
        P("fsdp", None),
        P("fsdp"),
        P(("fsdp", "rep"), "ctx", None),
    )
    return jax.shard_map(
        shards,
        mesh=mesh,
        in_specs=placed,
        out_specs=(
            P(("fsdp", "rep"), "ctx", None),
            P(("fsdp", "rep"), "ctx", None),
            P("fsdp"),
            P("fsdp"),
            P("fsdp", None),
            P("fsdp"),
            P("fsdp", None),
            P("fsdp"),
            P("fsdp"),
            P("fsdp"),
            P("fsdp", None),
            P("fsdp"),
            P("fsdp", None),
            P("fsdp"),
        ),
        check_vma=False,
    )
```

```python
import jax
import jax.numpy as jnp
from jax import lax
from jax.experimental import pallas as pl
from jax.experimental.pallas import tpu as pltpu
from jax.sharding import PartitionSpec as P

HD=64
QB=256
LOG2E=1.4426950408889634
NEG=-1e30

def dot_nn(a,b): return lax.dot_general(a,b,(((1,),(0,)),((),())),preferred_element_type=jnp.float32)
def dot_nt(a,b): return lax.dot_general(a,b,(((1,),(1,)),((),())),preferred_element_type=jnp.float32)
def dot_tn(a,b): return lax.dot_general(a,b,(((0,),(0,)),((),())),preferred_element_type=jnp.float32)

def key_extent(total, block):
    return max(total // 2, (block + 1) * QB)

def scores_t(keys, query, block, prefix, scale):
    raw = dot_nn(keys, query) * scale
    extent = raw.shape[0]
    free = block * QB
    if free:
        top, low = raw[:free], raw[free:]
    else:
        top, low = None, raw
    kpos = free + lax.broadcasted_iota(jnp.int32, low.shape, 0)
    qpos = free + lax.broadcasted_iota(jnp.int32, low.shape, 1)
    limit = jnp.maximum(qpos, prefix - 1)
    low = jnp.where(kpos <= limit, low, NEG)
    return low if top is None else jnp.concatenate([top, low], axis=0)

def fwd_kernel(info, q_ref, k_ref, v_ref, o_ref, l_ref):
    prefix = info[2]
    total = q_ref.shape[-1]
    keys = jnp.transpose(k_ref[0].astype(jnp.float32)).astype(jnp.bfloat16)
    scale = HD ** -0.5 * LOG2E
    for b in range(total // QB):
        ext = key_extent(total, b)
        sl = slice(b * QB, (b + 1) * QB)
        s = scores_t(keys[:ext], q_ref[0, :, sl], b, prefix, scale)
        top = jnp.max(s, axis=0, keepdims=True)
        p = jnp.exp2(s - top)
        denom = jnp.sum(p, axis=0, keepdims=True)
        mixed = dot_nn(v_ref[0, :, :ext], p.astype(jnp.bfloat16))
        o_ref[0, :, sl] = (mixed / denom).astype(jnp.bfloat16)
        l_ref[0, :, sl] = top + jnp.log2(denom)

def bwd_kernel(info, q_ref, k_ref, v_ref, o_ref, g_ref, l_ref, out_ref, dk_acc, dv_acc):
    prefix = info[2]
    total = q_ref.shape[-1]
    factor = HD ** -0.5
    scale = factor * LOG2E
    keep = jnp.where((info[3] == 0) & (pl.program_id(0) == pl.num_programs(0) - 1), 0.0, 1.0).astype(jnp.float32)
    keys_t = k_ref[0]
    keys = jnp.transpose(keys_t.astype(jnp.float32)).astype(jnp.bfloat16)
    values = jnp.transpose(v_ref[0].astype(jnp.float32)).astype(jnp.bfloat16)
    dk_acc[...] = jnp.zeros_like(dk_acc)
    dv_acc[...] = jnp.zeros_like(dv_acc)
    for b in range(total // QB):
        ext = key_extent(total, b)
        sl = slice(b * QB, (b + 1) * QB)
        query = q_ref[0, :, sl]
        grad = g_ref[0, :, sl]
        delta = jnp.sum(grad.astype(jnp.float32) * o_ref[0, :, sl].astype(jnp.float32), axis=0, keepdims=True)
        s = scores_t(keys[:ext], query, b, prefix, scale)
        p = jnp.exp2(s - l_ref[0, :, sl])
        dp = dot_nn(values[:ext], grad)
        ds = (p * (dp - delta)).astype(jnp.bfloat16)
        dv_acc[:, :ext] += dot_nt(grad, p.astype(jnp.bfloat16))
        dk_acc[:, :ext] += dot_nt(query, ds)
        out_ref[info[0], 0, :, sl] = (dot_nn(keys_t[:, :ext], ds) * (factor * keep)).astype(jnp.bfloat16)
    out_ref[1, 0] = (dk_acc[...] * (factor * keep)).astype(jnp.bfloat16)
    out_ref[info[1], 0] = (dv_acc[...] * keep).astype(jnp.bfloat16)

def attend(proj, info, heads):
    total = proj.shape[-1]
    cube = proj.reshape(3 * heads, HD, total)
    blk = lambda f: pl.BlockSpec((1, HD, total), f)
    cost = pl.CostEstimate(flops=4*heads*total*total*HD, bytes_accessed=8*heads*HD*total, transcendentals=heads*total*total)
    return pl.pallas_call(
        fwd_kernel,
        out_shape=(jax.ShapeDtypeStruct((heads, HD, total), jnp.bfloat16), jax.ShapeDtypeStruct((heads, 1, total), jnp.float32)),
        grid_spec=pltpu.PrefetchScalarGridSpec(num_scalar_prefetch=1, grid=(heads,),
            in_specs=[blk(lambda h, i: (i[0]*heads+h,0,0)), blk(lambda h, i: (heads+h,0,0)), blk(lambda h, i: (i[1]*heads+h,0,0))],
            out_specs=[blk(lambda h, i: (h,0,0)), pl.BlockSpec((1,1,total), lambda h,i:(h,0,0))]),
        cost_estimate=cost, name="attend")(info, cube, cube, cube)

def attend_back(proj, info, mixed, grad, logs, heads):
    total = proj.shape[-1]
    cube = proj.reshape(3 * heads, HD, total)
    blk = lambda f: pl.BlockSpec((1, HD, total), f)
    own = lambda h, i: (h,0,0)
    cost = pl.CostEstimate(flops=10*heads*total*total*HD, bytes_accessed=16*heads*HD*total, transcendentals=heads*total*total)
    return pl.pallas_call(
        bwd_kernel,
        out_shape=jax.ShapeDtypeStruct((3, heads, HD, total), jnp.bfloat16),
        grid_spec=pltpu.PrefetchScalarGridSpec(num_scalar_prefetch=1, grid=(heads,),
            in_specs=[blk(lambda h, i: (i[0]*heads+h,0,0)), blk(lambda h, i: (heads+h,0,0)), blk(lambda h, i: (i[1]*heads+h,0,0)), blk(own), blk(own), pl.BlockSpec((1,1,total), own)],
            out_specs=pl.BlockSpec((3,1,HD,total), lambda h,i:(0,h,0,0)),
            scratch_shapes=[pltpu.VMEM((HD,total),jnp.float32)]*2),
        cost_estimate=cost, name="attend_back")(info, cube, cube, cube, mixed, grad, logs)


EPS = 1e-05
BF = jnp.bfloat16
F32 = jnp.float32


def product(left, right, left_dim, right_dim):
    return lax.dot_general(
        left, right, (((left_dim,), (right_dim,)), ((), ())), preferred_element_type=F32
    )


def moments(values):
    center = values - jnp.mean(values, axis=-1, keepdims=True)
    variance = jnp.mean(center * center, axis=-1, keepdims=True)
    inverse = lax.rsqrt(variance + EPS)
    return center * inverse, inverse


def norm_backward(grad, scaled, inverse, gain):
    inner = grad * gain
    return inverse * (
        inner
        - jnp.mean(inner, axis=-1, keepdims=True)
        - scaled * jnp.mean(inner * scaled, axis=-1, keepdims=True)
    )


def hold(values, *after):
    return lax.optimization_barrier((values, after))[0]


def assemble(info, arrays, jobs, shape):
    total, rows = len(arrays), shape[1]

    def kernel(info_ref, *refs):
        out, sems = refs[total], refs[total + 1]

        def span(column, size):
            if isinstance(column, tuple):
                return pl.ds(pl.multiple_of(info_ref[column[0]], 128), size)
            return slice(column, column + size)

        copies = [
            pltpu.make_async_copy(
                refs[place].at[(*lead, slice(0, rows), span(source, size))],
                out.at[info_ref[block], :, span(target, size)],
                sems.at[i],
            )
            for i, (place, lead, block, source, target, size) in enumerate(jobs)
        ]
        for copy in copies:
            copy.start()
        for copy in copies:
            copy.wait()

    anywhere = pl.BlockSpec(memory_space=pl.ANY)
    return pl.pallas_call(
        kernel,
        out_shape=jax.ShapeDtypeStruct(shape, arrays[0].dtype),
        grid_spec=pltpu.PrefetchScalarGridSpec(
            num_scalar_prefetch=1,
            grid=(1,),
            in_specs=[anywhere] * total,
            out_specs=pl.BlockSpec(shape, lambda i, s: (0, 0, 0)),
            scratch_shapes=[pltpu.SemaphoreType.DMA((len(jobs),))],
        ),
        cost_estimate=pl.CostEstimate(
            flops=0, bytes_accessed=4 * shape[0] * shape[1] * shape[2], transcendentals=0
        ),
        name="assemble",
    )(info, *arrays)


def finish_pair(info, own, other, count, up_wide, skip):
    rows, total = own[0].shape
    wide = total - up_wide
    slab = (up_wide + up_wide // 128 * 128 - 128) // count
    up_skip = slab * count - up_wide

    def kernel(info_ref, a_ref, b_ref, c_ref, d_ref, up_ref, out_ref):
        flip, turn = info_ref[0] == 1, info_ref[1] == 1

        def both(x, y, take):
            x, y = x[...].astype(F32), y[...].astype(F32)
            low, high = jnp.where(flip, y, x), jnp.where(flip, x, y)
            ups = jnp.concatenate([low[:, :up_skip], high[:, :up_wide]], axis=1)
            return ups, x[:, up_wide:] + y[:, up_wide:]

        own_up, own_out = both(a_ref, b_ref, 0)
        other_up, other_out = both(c_ref, d_ref, 1)
        up_low, up_high = jnp.where(turn, other_up, own_up), jnp.where(turn, own_up, other_up)
        for p in range(count):
            at = slice(p * slab, (p + 1) * slab)
            up_ref[:, 2 * p * slab : (2 * p + 1) * slab] = up_low[:, at]
            up_ref[:, (2 * p + 1) * slab : (2 * p + 2) * slab] = up_high[:, at]
        out_ref[:, :skip] = jnp.where(turn, other_out, own_out)[:, :skip]
        out_ref[:, skip:] = jnp.where(turn, own_out, other_out)

    return pl.pallas_call(
        kernel,
        out_shape=(
            jax.ShapeDtypeStruct((rows, 2 * slab * count), F32),
            jax.ShapeDtypeStruct((rows, skip + wide), F32),
        ),
        grid_spec=pltpu.PrefetchScalarGridSpec(
            num_scalar_prefetch=1,
            grid=(1,),
            in_specs=[pl.BlockSpec((rows, total), lambda i, s: (0, 0))] * 4,
            out_specs=(
                pl.BlockSpec((rows, 2 * slab * count), lambda i, s: (0, 0)),
                pl.BlockSpec((rows, skip + wide), lambda i, s: (0, 0)),
            ),
        ),
        cost_estimate=pl.CostEstimate(
            flops=0, bytes_accessed=8 * rows * total + 8 * rows * slab * count, transcendentals=0
        ),
        name="finish_pair",
    )(info, *own, *other)


def finish_down(info, own, other):
    rows, width = own[0].shape

    def kernel(info_ref, a_ref, b_ref, c_ref, d_ref, out_ref):
        turn = info_ref[1] == 1
        mine = a_ref[...].astype(F32) + b_ref[...].astype(F32)
        theirs = c_ref[...].astype(F32) + d_ref[...].astype(F32)
        out_ref[:rows] = jnp.where(turn, theirs, mine)
        out_ref[rows:] = jnp.where(turn, mine, theirs)

    return pl.pallas_call(
        kernel,
        out_shape=jax.ShapeDtypeStruct((2 * rows, width), F32),
        grid_spec=pltpu.PrefetchScalarGridSpec(
            num_scalar_prefetch=1,
            grid=(1,),
            in_specs=[pl.BlockSpec((rows, width), lambda i, s: (0, 0))] * 4,
            out_specs=pl.BlockSpec((2 * rows, width), lambda i, s: (0, 0)),
        ),
        cost_estimate=pl.CostEstimate(
            flops=0, bytes_accessed=16 * rows * width, transcendentals=0
        ),
        name="finish_down",
    )(info, *own, *other)


class Grid:
    def __init__(self):
        self.count = lax.axis_size("fsdp")
        self.near = 1 << ((self.count.bit_length() - 1) // 2)
        self.far = self.count // self.near
        self.reps = lax.axis_size("rep")
        self.split = self.reps == 2 and self.near == 2
        place = lax.axis_index("fsdp")
        self.zi = place // self.near
        self.xi = place % self.near
        self.y = lax.axis_index("rep")
        self.c = lax.axis_index("ctx")
        order = [k for pair in zip(range(1, self.far), range(self.far - 1, 0, -1)) for k in pair]
        self.steps = list(dict.fromkeys(order))

    def far_shift(self, array, k):
        near, far = self.near, self.far
        pairs = [(i, (i // near + k) % far * near + i % near) for i in range(self.count)]
        return lax.ppermute(array, "fsdp", pairs)

    def near_shift(self, array, k):
        near = self.near
        pairs = [(i, i // near * near + (i % near + k) % near) for i in range(self.count)]
        return lax.ppermute(array, "fsdp", pairs)

    def swap_rep(self, array):
        return lax.ppermute(array, "rep", [(0, 1), (1, 0)])

    def swap_ctx(self, array):
        return lax.ppermute(array, "ctx", [(0, 1), (1, 0)])

    def lines(self, piece):
        return [piece] + [self.far_shift(piece, k) for k in range(1, self.far)]

    def spots(self):
        return [
            (self.zi - k) % self.far * self.near + (self.xi - j) % self.near
            for j in range(self.near)
            for k in range(self.far)
        ]

    def gather_all(self, piece):
        return lax.all_gather(piece, "fsdp", axis=0, tiled=True)

    def scatter_all(self, grads):
        return lax.psum_scatter(grads, "fsdp", scatter_dimension=0, tiled=True)

    def groups(self):
        steps = sorted(range(1, self.far), key=lambda k: (abs(2 * k - self.far), k)) + [0]
        return steps[: self.far // 2], steps[self.far // 2 :]

    def pick_lines(self, cube, steps):
        return jnp.stack(
            [
                lax.dynamic_index_in_dim(cube, (self.zi + k) % self.far, 0, keepdims=False)
                for k in steps
            ]
        )

    def near_send(self, cube):
        return self.near_shift(
            lax.dynamic_index_in_dim(cube, (self.xi + 1) % self.near, 1, keepdims=False), 1
        )

    def line_sum(self, cube, arrived, at):
        tail = cube.shape[2:]
        own = lax.dynamic_slice(cube, (at, self.xi, 0, 0), (1, 1, *tail)).reshape(tail)
        other = lax.dynamic_index_in_dim(arrived, at, 0, keepdims=False)
        return own.astype(F32) + other.astype(F32)

    def near_sum(self, cube, arrived, k):
        return self.line_sum(cube, arrived, (self.zi + k) % self.far)

    def scatter(self, grads):
        cube = grads.reshape(self.far, self.near, *grads.shape[1:])
        arrived = self.near_send(cube)
        passed = [
            self.far_shift(self.near_sum(cube, arrived, k).astype(grads.dtype), k)
            for k in range(1, self.far)
        ]
        total = self.near_sum(cube, arrived, 0)
        for extra in passed:
            total += extra.astype(F32)
        return total

    def sum_rep(self, total):
        if self.split:
            return total.astype(F32) + self.swap_rep(total.astype(BF)).astype(F32)
        return lax.psum(total.astype(F32), "rep")


def shards(
    tokens,
    prefix_len,
    ln1_gain,
    ln1_bias,
    w_qkv,
    b_qv,
    w_out,
    b_out,
    ln2_gain,
    ln2_bias,
    w_up,
    b_up,
    w_down,
    b_down,
    cotangent,
):
    grid = Grid()
    count, c, y = grid.count, grid.c, grid.y
    first = c == 0
    seqs, rows, width = tokens.shape
    total_len = 2 * rows
    heads_all = width // HD
    heads = (heads_all + 1) // 2
    wide = heads * HD
    skip = width - wide
    part = width // count
    ff = w_up.shape[1]
    half_ff = ff // 2
    slab = ff // count // 2
    own_tokens = tokens.reshape(rows, width)
    own_cot = cotangent.reshape(rows, width)
    lead = (y == 0) if grid.split else True

    def choose(flag, a, b):
        return a if flag is True else jnp.where(flag, a, b)

    def both(own, other):
        return jnp.where(
            first,
            jnp.concatenate([own, other], axis=0),
            jnp.concatenate([other, own], axis=0),
        )

    small = [ln1_gain, ln1_bias, b_qv, b_out, ln2_gain, ln2_bias, b_up, b_down]
    sizes = [v.shape[0] for v in small]

    def section(k):
        low = w_qkv[:, k * width : k * width + wide]
        return jnp.where(first, low, w_qkv[:, k * width + skip : k * width + skip + wide])

    w_q, w_k, w_v = section(0), section(1), section(2)
    down_own = lax.dynamic_slice(w_down, (slab * c, 0), (slab, width))
    out_own = lax.dynamic_slice(w_out, (0, skip * c), (part, wide))
    up_cols = w_up.reshape(part, count, 2, slab)
    up_own = lax.dynamic_index_in_dim(up_cols, c, 2, keepdims=False).reshape(part, half_ff)
    up_skip = half_ff // 2 // 128 * 128
    up_wide = half_ff - up_skip
    if grid.split:
        far = grid.far
        mine = jnp.where(lead, w_q, w_v)
        tail = jnp.stack([jnp.pad(v, (0, 2 * wide - v.shape[0])) for v in small])
        lines = grid.lines(
            jnp.concatenate([jnp.concatenate([mine, w_k], axis=1), tail], axis=0)
        )
        up_cut = lambda rep: lax.dynamic_slice(up_own, (0, up_skip * rep), (part, up_wide))
        lines, up_mine, out_own, down_own = hold((lines, up_cut(y), out_own, down_own))
        half_out = grid.gather_all(out_own)
        full_down = grid.gather_all(down_own)
        qkv_near = jnp.stack(lines)
        qkv_next = grid.near_shift(qkv_near, 1)
        up_lines = grid.lines(up_mine)
        qkv_near, qkv_next, up_lines = hold((qkv_near, qkv_next, up_lines))
        qkv_other = grid.swap_rep(
            jnp.stack([qkv_near[:, :part, :wide], qkv_next[:, :part, :wide]])
        )
        up_near = jnp.stack(up_lines)
        up_next = grid.near_shift(up_near, 1)
        spots = jnp.stack(
            grid.spots() + [up_skip * y, (up_wide - up_skip) * (1 - y), up_wide * (1 - y)]
        ).astype(jnp.int32)
        tails = jnp.concatenate([qkv_near[:, part:, : max(sizes)], qkv_next[:, part:, : max(sizes)]])
        chosen = spots[None, :count, None, None] == jnp.arange(count)[:, None, None, None]
        tails = jnp.sum(jnp.where(chosen, tails[None].astype(F32), 0.0), axis=1)
        small_full = [tails[:, i, :size].reshape(-1) for i, size in enumerate(sizes)]
    else:
        small_full = [grid.gather_all(v).astype(F32) for v in small]
        half_out = grid.gather_all(out_own)
        full_up = grid.gather_all(up_own)
        full_down = grid.gather_all(down_own)
    gain_one, shift_one, bias_qv, bias_out, gain_two, shift_two, bias_up, bias_down = small_full

    all_tokens = both(own_tokens, grid.swap_ctx(own_tokens))
    all_cot = both(own_cot, grid.swap_ctx(own_cot))
    inputs = all_tokens.astype(F32)
    scaled_one, _ = moments(inputs)
    normed = (scaled_one * gain_one + shift_one).astype(BF)
    if grid.split:
        qkv_near, qkv_next, qkv_other, up_near, up_next, normed = hold(
            (qkv_near, qkv_next, qkv_other, up_near, up_next, normed)
        )
        full_qkv = assemble(
            spots,
            [qkv_near, qkv_next, qkv_other],
            [(i // far, (i % far,), i, 0, 0, 2 * wide) for i in range(count)]
            + [(2, (i // far, i % far), i, 0, 2 * wide, wide) for i in range(count)],
            (count, part, 3 * wide),
        )
        up_other = grid.swap_rep(jnp.stack([up_near, up_next]))
    else:
        full_qkv = grid.gather_all(jnp.concatenate([w_q, w_k, w_v], axis=1))
    full_qkv = full_qkv.reshape(width, 3 * wide)

    bias_q = lax.dynamic_slice(bias_qv, (skip * c,), (wide,))
    bias_v = lax.dynamic_slice(bias_qv, (width + skip * c,), (wide,))
    bias_row = jnp.concatenate(
        [choose(lead, bias_q, bias_v), jnp.zeros((wide,), F32), choose(lead, bias_v, bias_q)]
    )
    project = (product(full_qkv, normed, 0, 1) + bias_row[:, None]).astype(BF)
    flip = jnp.int32(0) if lead is True else jnp.where(lead, 0, 2).astype(jnp.int32)
    info = jnp.stack([flip, 2 - flip, prefix_len[0], c.astype(jnp.int32)])
    mixed, logs = attend(project, info, heads)
    other_out = grid.swap_ctx(half_out)
    full_out = jnp.concatenate(
        [jnp.where(first, half_out, other_out)[:, :skip], jnp.where(first, other_out, half_out)],
        axis=1,
    )
    bias_up_own = lax.dynamic_index_in_dim(bias_up.reshape(count, 2, slab), c, 1, keepdims=False)
    bias_up_own = bias_up_own.reshape(half_ff)
    own_mixed = mixed.reshape(wide, total_len)
    other_mixed = grid.swap_ctx(own_mixed)
    overlap = wide - skip
    attended = jnp.where(
        first,
        jnp.concatenate([own_mixed, other_mixed[overlap:]], axis=0),
        jnp.concatenate([other_mixed, own_mixed[overlap:]], axis=0),
    )

    middle = inputs + product(attended, full_out, 0, 0) + bias_out
    if grid.split:
        middle, up_other = hold((middle, up_other))
        full_up = assemble(
            spots,
            [up_near, up_next, up_other],
            [(i // far, (i % far,), i, 0, (count,), up_wide) for i in range(count)]
            + [
                (2, (i // far, i % far), i, (count + 1,), (count + 2,), up_skip)
                for i in range(count)
            ],
            (count, part, half_ff),
        ).reshape(width, half_ff)
    scaled_two, inverse_two = moments(middle)
    hidden_in = (scaled_two * gain_two + shift_two).astype(BF)
    pre = product(hidden_in, full_up, 1, 0) + bias_up_own
    cdf = 0.5 + 0.5 * lax.erf(pre * (0.5**0.5))
    activated = (pre * cdf).astype(BF)
    slope = (cdf + pre * jnp.exp(-0.5 * pre * pre) * (0.5 / jnp.pi) ** 0.5).astype(BF)

    own_rows = lambda array: lax.dynamic_slice(array, (rows * c, 0), (rows, array.shape[1]))
    other_rows = lambda array: lax.dynamic_slice(
        array, (rows * (1 - c), 0), (rows, array.shape[1])
    )

    grad_down = product(activated, all_cot, 0, 0).astype(BF)
    full_down, grad_down = hold((full_down, grad_down))
    grad_act = product(all_cot, full_down, 1, 1)
    grad_pre = (grad_act * slope.astype(F32)).astype(BF)
    if grid.split:
        own_down = grid.scatter_all(grad_down)
        grad_cut = lambda rep: lax.dynamic_slice(grad_pre, (0, up_skip * rep), (total_len, up_wide))
        up_sent = product(hidden_in, grad_cut(1 - y), 0, 0).astype(BF)
        up_mine = product(hidden_in, grad_cut(y), 0, 0).astype(BF)
        rows_cube = lambda g: g.reshape(far, grid.near, part, g.shape[1])
        groups = grid.groups()
        up_sent, up_mine = rows_cube(up_sent), rows_cube(up_mine)
        up_sent = [grid.swap_rep(grid.pick_lines(up_sent, steps)) for steps in groups]
    else:
        own_down = grid.scatter_all(grad_down)
        grad_up = product(hidden_in, grad_pre, 0, 0).astype(BF)
    grad_hidden = product(grad_pre, full_up, 1, 1)
    partial_down = product(activated, full_down, 1, 0)
    result = own_rows(partial_down) + grid.swap_ctx(other_rows(partial_down))
    block_out = (own_rows(middle) + result + bias_down).astype(BF).reshape(seqs, rows, width)
    grad_hidden = grad_hidden + grid.swap_ctx(grad_hidden)
    if grid.split:
        grad_hidden, up_mine, up_sent[0], block_out = hold(
            (grad_hidden, up_mine, up_sent[0], block_out)
        )
        merge = lambda i: (
            grid.pick_lines(up_mine, groups[i]).astype(F32) + up_sent[i].astype(F32)
        ).astype(BF)
        up_cubes = [merge(0)]
        up_near = [grid.near_send(up_cubes[0])]
    grad_middle = all_cot.astype(F32) + norm_backward(grad_hidden, scaled_two, inverse_two, gain_two)
    grad_branch = grad_middle.astype(BF)
    if grid.split:
        grad_branch, up_near, up_cubes, block_out = hold(
            (grad_branch, up_near, up_cubes, block_out)
        )
        send_far = lambda i: {
            k: grid.far_shift(grid.line_sum(up_cubes[i], up_near[i], at).astype(BF), k)
            for at, k in enumerate(groups[i])
            if k
        }
        up_far = send_far(0)
    branch_cols = lax.dynamic_slice(grad_branch, (0, skip * c), (total_len, wide))
    grad_wout = product(attended, branch_cols, 1, 0).astype(BF)
    out_rows = lax.dynamic_slice(full_out, (skip * c, 0), (wide, width))
    grad_mixed = product(out_rows, grad_branch, 1, 1).astype(BF).reshape(heads, HD, total_len)
    if grid.split:
        up_sent[1], grad_wout, grad_mixed = hold((up_sent[1], grad_wout, grad_mixed))
        up_cubes.append(merge(1))
        up_near.append(grid.near_send(up_cubes[1]))
        out_cube = rows_cube(grad_wout)
        out_near = grid.near_send(out_cube)
    grad_cube = attend_back(project, info, mixed, grad_mixed, logs, heads)
    if grid.split:
        grad_cube, up_near, up_cubes, up_far, out_near, out_cube = hold(
            (grad_cube, up_near, up_cubes, up_far, out_near, out_cube)
        )
        up_far.update(send_far(1))
        out_far = [
            grid.far_shift(grid.near_sum(out_cube, out_near, k).astype(BF), k)
            for k in range(1, far)
        ]
    grad_project = grad_cube.reshape(3 * wide, total_len)
    qkv_sent = product(normed, grad_project[2 * wide :], 0, 1).astype(BF)
    if grid.split:
        qkv_keys = product(normed, grad_project[wide : 2 * wide], 0, 1).astype(BF)
        qkv_mine = product(normed, grad_project[:wide], 0, 1).astype(BF)
    else:
        qkv_mine = product(normed, grad_project[: 2 * wide], 0, 1).astype(BF)
    if grid.split:
        qkv_sent, qkv_mine, qkv_keys, grad_project = hold(
            (qkv_sent, qkv_mine, qkv_keys, grad_project)
        )
        qkv_sent = grid.swap_rep(qkv_sent)
        key_cube = rows_cube(qkv_keys)
        key_near = grid.near_send(key_cube)
    grad_normed = product(grad_project, full_qkv, 0, 1)
    if grid.split:
        qkv_sent, qkv_mine, key_near, key_cube, grad_normed = hold(
            (qkv_sent, qkv_mine, key_near, key_cube, grad_normed)
        )
        low = qkv_mine.astype(F32) + qkv_sent.astype(F32)
        low_cube = rows_cube(low.astype(BF))
        low_near = grid.near_send(low_cube)
    own_grad = own_rows(grad_normed) + grid.swap_ctx(other_rows(grad_normed))
    own_scaled, own_inverse = moments(own_tokens.astype(F32))
    grad_tokens = own_rows(grad_middle) + norm_backward(own_grad, own_scaled, own_inverse, gain_one)
    grad_tokens = grad_tokens.reshape(seqs, rows, width)

    if grid.split:
        low_near, low_cube, key_near, key_cube, up_far, out_far, own_grad = hold(
            (low_near, low_cube, key_near, key_cube, up_far, out_far, own_grad)
        )
        key_far = [
            grid.far_shift(grid.near_sum(key_cube, key_near, k).astype(BF), k)
            for k in range(1, far)
        ]
        up_total = grid.line_sum(up_cubes[1], up_near[1], far - far // 2 - 1)
        for extra in up_far.values():
            up_total += extra.astype(F32)
        out_total = grid.near_sum(out_cube, out_near, 0)
        for extra in out_far:
            out_total += extra.astype(F32)
        pair = jnp.concatenate([up_total.astype(BF), out_total.astype(BF)], axis=1)
        low_far = [
            grid.far_shift(grid.near_sum(low_cube, low_near, k).astype(BF), k)
            for k in range(1, far)
        ]
        pair_other = grid.swap_rep(pair)
        places = jnp.stack([y, c]).astype(jnp.int32)
        out_up, out_wout = finish_pair(
            places,
            (pair, pair_other),
            (grid.swap_ctx(pair), grid.swap_ctx(pair_other)),
            count,
            up_wide,
            skip,
        )
        down_other = grid.swap_rep(own_down)
        out_down = finish_down(
            places,
            (own_down, down_other),
            (grid.swap_ctx(own_down), grid.swap_ctx(down_other)),
        )
    else:
        own_down = grid.sum_rep(own_down).astype(BF)
        other_down = grid.swap_ctx(own_down)
        out_down = jnp.where(
            first,
            jnp.concatenate([own_down, other_down], axis=0),
            jnp.concatenate([other_down, own_down], axis=0),
        ).astype(F32)
        own_up = grid.sum_rep(grid.scatter_all(grad_up)).astype(BF)
        other_up = grid.swap_ctx(own_up)
        weave = lambda a, b: jnp.stack(
            [a.reshape(part, count, slab), b.reshape(part, count, slab)], axis=2
        ).reshape(part, ff)
        out_up = weave(
            jnp.where(first, own_up, other_up), jnp.where(first, other_up, own_up)
        ).astype(F32)
        own_wout = grid.sum_rep(grid.scatter_all(grad_wout)).astype(BF)
        other_wout = grid.swap_ctx(own_wout)
        out_wout = jnp.concatenate(
            [
                jnp.where(first, own_wout, other_wout)[:, :skip],
                jnp.where(first, other_wout, own_wout),
            ],
            axis=1,
        ).astype(F32)

    if grid.split:
        keys = grid.near_sum(key_cube, key_near, 0)
        for extra in key_far:
            keys += extra.astype(F32)
        centre = grid.sum_rep(keys).astype(BF)
        low_far, out_up, out_wout, out_down, centre = hold(
            (low_far, out_up, out_wout, out_down, centre)
        )
        mine = grid.near_sum(low_cube, low_near, 0)
        for extra in low_far:
            mine += extra.astype(F32)
        mine = mine.astype(BF)
        other = grid.swap_rep(mine)
        own_sections = [
            jnp.where(lead, mine, other),
            centre,
            jnp.where(lead, other, mine),
        ]
    else:
        own_qkv = [grid.sum_rep(grid.scatter_all(g)).astype(BF) for g in (qkv_mine, qkv_sent)]
        own_sections = [own_qkv[0][:, :wide], own_qkv[0][:, wide:], own_qkv[1]]
    own_qkv = jnp.concatenate(own_sections, axis=1)
    other_qkv = grid.swap_ctx(own_qkv)
    low_qkv = jnp.where(first, own_qkv, other_qkv)
    high_qkv = jnp.where(first, other_qkv, own_qkv)
    pieces = []
    for k in range(3):
        pieces.append(low_qkv[:, k * wide : k * wide + skip])
        pieces.append(high_qkv[:, k * wide : (k + 1) * wide])
    out_qkv = jnp.concatenate(pieces, axis=1).astype(F32)

    once = jnp.where(first, 1.0, 0.0).astype(F32)
    spread = lambda values, start, size: lax.dynamic_update_slice(
        jnp.zeros((size,), F32), values, (start,)
    )
    project_sums = jnp.sum(grad_cube.astype(F32), axis=3).reshape(3, wide)
    sums_q = choose(lead, project_sums[0], project_sums[2])
    sums_v = choose(lead, project_sums[2], project_sums[0])
    grad_bias_qv = jnp.concatenate(
        [spread(sums_q, skip * c, width), spread(sums_v, skip * c, width)]
    )
    pre_sums = jnp.sum(grad_pre.astype(F32), axis=0).reshape(count, slab)
    grad_bias_up = lax.dynamic_update_slice(
        jnp.zeros((count, 2, slab), F32), pre_sums[:, None], (0, c, 0)
    )
    vectors = [
        jnp.sum(own_grad * own_scaled, axis=0),
        jnp.sum(own_grad, axis=0),
        grad_bias_qv,
        once * jnp.sum(grad_branch.astype(F32), axis=0),
        once * jnp.sum(grad_hidden * scaled_two, axis=0),
        once * jnp.sum(grad_hidden, axis=0),
        grad_bias_up,
        once * jnp.sum(all_cot.astype(F32), axis=0),
    ]
    table = jnp.concatenate([v.reshape(count, -1) for v in vectors], axis=1)
    table = table + grid.swap_ctx(table)
    table = table + grid.swap_rep(table) if grid.split else lax.psum(table, "rep")
    summed = grid.scatter(table[:, None, :]).reshape(-1)
    outs, at = [], 0
    for size in sizes:
        outs.append(summed[at : at + size])
        at += size
    return (
        block_out,
        grad_tokens,
        outs[0],
        outs[1],
        out_qkv,
        outs[2],
        out_wout,
        outs[3],
        outs[4],
        outs[5],
        out_up,
        outs[6],
        out_down,
        outs[7],
    )


def solution(mesh):
    placed = (
        P(("fsdp", "rep"), "ctx", None),
        P(("fsdp", "rep")),
        P("fsdp"),
        P("fsdp"),
        P("fsdp", None),
        P("fsdp"),
        P("fsdp", None),
        P("fsdp"),
        P("fsdp"),
        P("fsdp"),
        P("fsdp", None),
        P("fsdp"),
        P("fsdp", None),
        P("fsdp"),
        P(("fsdp", "rep"), "ctx", None),
    )
    return jax.shard_map(
        shards,
        mesh=mesh,
        in_specs=placed,
        out_specs=(
            P(("fsdp", "rep"), "ctx", None),
            P(("fsdp", "rep"), "ctx", None),
            P("fsdp"),
            P("fsdp"),
            P("fsdp", None),
            P("fsdp"),
            P("fsdp", None),
            P("fsdp"),
            P("fsdp"),
            P("fsdp"),
            P("fsdp", None),
            P("fsdp"),
            P("fsdp", None),
            P("fsdp"),
        ),
        check_vma=False,
    )
```

```python
import jax
import jax.numpy as jnp
from jax import lax
from jax.experimental import pallas as pl
from jax.experimental.pallas import tpu as pltpu
from jax.sharding import PartitionSpec as P

HD=64
QB=256
LOG2E=1.4426950408889634
NEG=-1e30

def dot_nn(a,b): return lax.dot_general(a,b,(((1,),(0,)),((),())),preferred_element_type=jnp.float32)
def dot_nt(a,b): return lax.dot_general(a,b,(((1,),(1,)),((),())),preferred_element_type=jnp.float32)
def dot_tn(a,b): return lax.dot_general(a,b,(((0,),(0,)),((),())),preferred_element_type=jnp.float32)

def key_extent(total, block):
    return max(total // 2, (block + 1) * QB)

def scores_t(keys, query, block, prefix, scale):
    raw = dot_nn(keys, query) * scale
    extent = raw.shape[0]
    free = block * QB
    if free:
        top, low = raw[:free], raw[free:]
    else:
        top, low = None, raw
    kpos = free + lax.broadcasted_iota(jnp.int32, low.shape, 0)
    qpos = free + lax.broadcasted_iota(jnp.int32, low.shape, 1)
    limit = jnp.maximum(qpos, prefix - 1)
    low = jnp.where(kpos <= limit, low, NEG)
    return low if top is None else jnp.concatenate([top, low], axis=0)

def fwd_kernel(info, q_ref, k_ref, v_ref, o_ref, l_ref):
    prefix = info[2]
    total = q_ref.shape[-1]
    keys = jnp.transpose(k_ref[0].astype(jnp.float32)).astype(jnp.bfloat16)
    scale = HD ** -0.5 * LOG2E
    for b in range(total // QB):
        ext = key_extent(total, b)
        sl = slice(b * QB, (b + 1) * QB)
        s = scores_t(keys[:ext], q_ref[0, :, sl], b, prefix, scale)
        top = jnp.max(s, axis=0, keepdims=True)
        p = jnp.exp2(s - top)
        denom = jnp.sum(p, axis=0, keepdims=True)
        mixed = dot_nn(v_ref[0, :, :ext], p.astype(jnp.bfloat16))
        o_ref[0, :, sl] = (mixed / denom).astype(jnp.bfloat16)
        l_ref[0, :, sl] = top + jnp.log2(denom)

def bwd_kernel(info, q_ref, k_ref, v_ref, o_ref, g_ref, l_ref, out_ref, dk_acc, dv_acc):
    prefix = info[2]
    total = q_ref.shape[-1]
    factor = HD ** -0.5
    scale = factor * LOG2E
    keep = jnp.where((info[3] == 0) & (pl.program_id(0) == pl.num_programs(0) - 1), 0.0, 1.0).astype(jnp.float32)
    keys_t = k_ref[0]
    keys = jnp.transpose(keys_t.astype(jnp.float32)).astype(jnp.bfloat16)
    values = jnp.transpose(v_ref[0].astype(jnp.float32)).astype(jnp.bfloat16)
    dk_acc[...] = jnp.zeros_like(dk_acc)
    dv_acc[...] = jnp.zeros_like(dv_acc)
    for b in range(total // QB):
        ext = key_extent(total, b)
        sl = slice(b * QB, (b + 1) * QB)
        query = q_ref[0, :, sl]
        grad = g_ref[0, :, sl]
        delta = jnp.sum(grad.astype(jnp.float32) * o_ref[0, :, sl].astype(jnp.float32), axis=0, keepdims=True)
        s = scores_t(keys[:ext], query, b, prefix, scale)
        p = jnp.exp2(s - l_ref[0, :, sl])
        dp = dot_nn(values[:ext], grad)
        ds = (p * (dp - delta)).astype(jnp.bfloat16)
        dv_acc[:, :ext] += dot_nt(grad, p.astype(jnp.bfloat16))
        dk_acc[:, :ext] += dot_nt(query, ds)
        out_ref[info[0], 0, :, sl] = (dot_nn(keys_t[:, :ext], ds) * (factor * keep)).astype(jnp.bfloat16)
    out_ref[1, 0] = (dk_acc[...] * (factor * keep)).astype(jnp.bfloat16)
    out_ref[info[1], 0] = (dv_acc[...] * keep).astype(jnp.bfloat16)

def attend(proj, info, heads):
    total = proj.shape[-1]
    cube = proj.reshape(3 * heads, HD, total)
    blk = lambda f: pl.BlockSpec((1, HD, total), f)
    cost = pl.CostEstimate(flops=4*heads*total*total*HD, bytes_accessed=8*heads*HD*total, transcendentals=heads*total*total)
    return pl.pallas_call(
        fwd_kernel,
        out_shape=(jax.ShapeDtypeStruct((heads, HD, total), jnp.bfloat16), jax.ShapeDtypeStruct((heads, 1, total), jnp.float32)),
        grid_spec=pltpu.PrefetchScalarGridSpec(num_scalar_prefetch=1, grid=(heads,),
            in_specs=[blk(lambda h, i: (i[0]*heads+h,0,0)), blk(lambda h, i: (heads+h,0,0)), blk(lambda h, i: (i[1]*heads+h,0,0))],
            out_specs=[blk(lambda h, i: (h,0,0)), pl.BlockSpec((1,1,total), lambda h,i:(h,0,0))]),
        cost_estimate=cost, name="attend")(info, cube, cube, cube)

def attend_back(proj, info, mixed, grad, logs, heads):
    total = proj.shape[-1]
    cube = proj.reshape(3 * heads, HD, total)
    blk = lambda f: pl.BlockSpec((1, HD, total), f)
    own = lambda h, i: (h,0,0)
    cost = pl.CostEstimate(flops=10*heads*total*total*HD, bytes_accessed=16*heads*HD*total, transcendentals=heads*total*total)
    return pl.pallas_call(
        bwd_kernel,
        out_shape=jax.ShapeDtypeStruct((3, heads, HD, total), jnp.bfloat16),
        grid_spec=pltpu.PrefetchScalarGridSpec(num_scalar_prefetch=1, grid=(heads,),
            in_specs=[blk(lambda h, i: (i[0]*heads+h,0,0)), blk(lambda h, i: (heads+h,0,0)), blk(lambda h, i: (i[1]*heads+h,0,0)), blk(own), blk(own), pl.BlockSpec((1,1,total), own)],
            out_specs=pl.BlockSpec((3,1,HD,total), lambda h,i:(0,h,0,0)),
            scratch_shapes=[pltpu.VMEM((HD,total),jnp.float32)]*2),
        cost_estimate=cost, name="attend_back")(info, cube, cube, cube, mixed, grad, logs)


EPS = 1e-05
BF = jnp.bfloat16
F32 = jnp.float32


def product(left, right, left_dim, right_dim):
    return lax.dot_general(
        left, right, (((left_dim,), (right_dim,)), ((), ())), preferred_element_type=F32
    )


def moments(values):
    center = values - jnp.mean(values, axis=-1, keepdims=True)
    variance = jnp.mean(center * center, axis=-1, keepdims=True)
    inverse = lax.rsqrt(variance + EPS)
    return center * inverse, inverse


def norm_backward(grad, scaled, inverse, gain):
    inner = grad * gain
    return inverse * (
        inner
        - jnp.mean(inner, axis=-1, keepdims=True)
        - scaled * jnp.mean(inner * scaled, axis=-1, keepdims=True)
    )


def hold(values, *after):
    return lax.optimization_barrier((values, after))[0]


def assemble(info, arrays, jobs, shape):
    total, rows = len(arrays), shape[1]

    def kernel(info_ref, *refs):
        out, sems = refs[total], refs[total + 1]

        def span(column, size):
            if isinstance(column, tuple):
                return pl.ds(pl.multiple_of(info_ref[column[0]], 128), size)
            return slice(column, column + size)

        copies = [
            pltpu.make_async_copy(
                refs[place].at[(*lead, slice(0, rows), span(source, size))],
                out.at[info_ref[block], :, span(target, size)],
                sems.at[i],
            )
            for i, (place, lead, block, source, target, size) in enumerate(jobs)
        ]
        for copy in copies:
            copy.start()
        for copy in copies:
            copy.wait()

    anywhere = pl.BlockSpec(memory_space=pl.ANY)
    return pl.pallas_call(
        kernel,
        out_shape=jax.ShapeDtypeStruct(shape, arrays[0].dtype),
        grid_spec=pltpu.PrefetchScalarGridSpec(
            num_scalar_prefetch=1,
            grid=(1,),
            in_specs=[anywhere] * total,
            out_specs=pl.BlockSpec(shape, lambda i, s: (0, 0, 0)),
            scratch_shapes=[pltpu.SemaphoreType.DMA((len(jobs),))],
        ),
        cost_estimate=pl.CostEstimate(
            flops=0, bytes_accessed=4 * shape[0] * shape[1] * shape[2], transcendentals=0
        ),
        name="assemble",
    )(info, *arrays)


def finish_pair(info, own, other, count, up_wide, skip):
    rows, total = own[0].shape
    wide = total - up_wide
    slab = (up_wide + up_wide // 128 * 128 - 128) // count
    up_skip = slab * count - up_wide

    def kernel(info_ref, a_ref, b_ref, c_ref, d_ref, up_ref, out_ref):
        flip, turn = info_ref[0] == 1, info_ref[1] == 1

        def both(x, y, take):
            x, y = x[...].astype(F32), y[...].astype(F32)
            low, high = jnp.where(flip, y, x), jnp.where(flip, x, y)
            ups = jnp.concatenate([low[:, :up_skip], high[:, :up_wide]], axis=1)
            return ups, x[:, up_wide:] + y[:, up_wide:]

        own_up, own_out = both(a_ref, b_ref, 0)
        other_up, other_out = both(c_ref, d_ref, 1)
        up_low, up_high = jnp.where(turn, other_up, own_up), jnp.where(turn, own_up, other_up)
        for p in range(count):
            at = slice(p * slab, (p + 1) * slab)
            up_ref[:, 2 * p * slab : (2 * p + 1) * slab] = up_low[:, at]
            up_ref[:, (2 * p + 1) * slab : (2 * p + 2) * slab] = up_high[:, at]
        out_ref[:, :skip] = jnp.where(turn, other_out, own_out)[:, :skip]
        out_ref[:, skip:] = jnp.where(turn, own_out, other_out)

    return pl.pallas_call(
        kernel,
        out_shape=(
            jax.ShapeDtypeStruct((rows, 2 * slab * count), F32),
            jax.ShapeDtypeStruct((rows, skip + wide), F32),
        ),
        grid_spec=pltpu.PrefetchScalarGridSpec(
            num_scalar_prefetch=1,
            grid=(1,),
            in_specs=[pl.BlockSpec((rows, total), lambda i, s: (0, 0))] * 4,
            out_specs=(
                pl.BlockSpec((rows, 2 * slab * count), lambda i, s: (0, 0)),
                pl.BlockSpec((rows, skip + wide), lambda i, s: (0, 0)),
            ),
        ),
        cost_estimate=pl.CostEstimate(
            flops=0, bytes_accessed=8 * rows * total + 8 * rows * slab * count, transcendentals=0
        ),
        name="finish_pair",
    )(info, *own, *other)


def finish_down(info, own, other):
    rows, width = own[0].shape

    def kernel(info_ref, a_ref, b_ref, c_ref, d_ref, out_ref):
        turn = info_ref[1] == 1
        mine = a_ref[...].astype(F32) + b_ref[...].astype(F32)
        theirs = c_ref[...].astype(F32) + d_ref[...].astype(F32)
        out_ref[:rows] = jnp.where(turn, theirs, mine)
        out_ref[rows:] = jnp.where(turn, mine, theirs)

    return pl.pallas_call(
        kernel,
        out_shape=jax.ShapeDtypeStruct((2 * rows, width), F32),
        grid_spec=pltpu.PrefetchScalarGridSpec(
            num_scalar_prefetch=1,
            grid=(1,),
            in_specs=[pl.BlockSpec((rows, width), lambda i, s: (0, 0))] * 4,
            out_specs=pl.BlockSpec((2 * rows, width), lambda i, s: (0, 0)),
        ),
        cost_estimate=pl.CostEstimate(
            flops=0, bytes_accessed=16 * rows * width, transcendentals=0
        ),
        name="finish_down",
    )(info, *own, *other)


class Grid:
    def __init__(self):
        self.count = lax.axis_size("fsdp")
        self.near = 1 << ((self.count.bit_length() - 1) // 2)
        self.far = self.count // self.near
        self.reps = lax.axis_size("rep")
        self.split = self.reps == 2 and self.near == 2
        place = lax.axis_index("fsdp")
        self.zi = place // self.near
        self.xi = place % self.near
        self.y = lax.axis_index("rep")
        self.c = lax.axis_index("ctx")
        order = [k for pair in zip(range(1, self.far), range(self.far - 1, 0, -1)) for k in pair]
        self.steps = list(dict.fromkeys(order))

    def far_shift(self, array, k):
        near, far = self.near, self.far
        pairs = [(i, (i // near + k) % far * near + i % near) for i in range(self.count)]
        return lax.ppermute(array, "fsdp", pairs)

    def near_shift(self, array, k):
        near = self.near
        pairs = [(i, i // near * near + (i % near + k) % near) for i in range(self.count)]
        return lax.ppermute(array, "fsdp", pairs)

    def swap_rep(self, array):
        return lax.ppermute(array, "rep", [(0, 1), (1, 0)])

    def swap_ctx(self, array):
        return lax.ppermute(array, "ctx", [(0, 1), (1, 0)])

    def lines(self, piece):
        return [piece] + [self.far_shift(piece, k) for k in range(1, self.far)]

    def spots(self):
        return [
            (self.zi - k) % self.far * self.near + (self.xi - j) % self.near
            for j in range(self.near)
            for k in range(self.far)
        ]

    def gather_all(self, piece):
        return lax.all_gather(piece, "fsdp", axis=0, tiled=True)

    def scatter_all(self, grads):
        return lax.psum_scatter(grads, "fsdp", scatter_dimension=0, tiled=True)

    def groups(self):
        steps = sorted(range(1, self.far), key=lambda k: (abs(2 * k - self.far), k)) + [0]
        return steps[: self.far // 2], steps[self.far // 2 :]

    def pick_lines(self, cube, steps):
        return jnp.stack(
            [
                lax.dynamic_index_in_dim(cube, (self.zi + k) % self.far, 0, keepdims=False)
                for k in steps
            ]
        )

    def near_send(self, cube):
        return self.near_shift(
            lax.dynamic_index_in_dim(cube, (self.xi + 1) % self.near, 1, keepdims=False), 1
        )

    def line_sum(self, cube, arrived, at):
        tail = cube.shape[2:]
        own = lax.dynamic_slice(cube, (at, self.xi, 0, 0), (1, 1, *tail)).reshape(tail)
        other = lax.dynamic_index_in_dim(arrived, at, 0, keepdims=False)
        return own.astype(F32) + other.astype(F32)

    def near_sum(self, cube, arrived, k):
        return self.line_sum(cube, arrived, (self.zi + k) % self.far)

    def scatter(self, grads):
        cube = grads.reshape(self.far, self.near, *grads.shape[1:])
        arrived = self.near_send(cube)
        passed = [
            self.far_shift(self.near_sum(cube, arrived, k).astype(grads.dtype), k)
            for k in range(1, self.far)
        ]
        total = self.near_sum(cube, arrived, 0)
        for extra in passed:
            total += extra.astype(F32)
        return total

    def sum_rep(self, total):
        if self.split:
            return total.astype(F32) + self.swap_rep(total.astype(BF)).astype(F32)
        return lax.psum(total.astype(F32), "rep")


def shards(
    tokens,
    prefix_len,
    ln1_gain,
    ln1_bias,
    w_qkv,
    b_qv,
    w_out,
    b_out,
    ln2_gain,
    ln2_bias,
    w_up,
    b_up,
    w_down,
    b_down,
    cotangent,
):
    grid = Grid()
    count, c, y = grid.count, grid.c, grid.y
    first = c == 0
    seqs, rows, width = tokens.shape
    total_len = 2 * rows
    heads_all = width // HD
    heads = (heads_all + 1) // 2
    wide = heads * HD
    skip = width - wide
    part = width // count
    ff = w_up.shape[1]
    half_ff = ff // 2
    slab = ff // count // 2
    own_tokens = tokens.reshape(rows, width)
    own_cot = cotangent.reshape(rows, width)
    lead = (y == 0) if grid.split else True

    def choose(flag, a, b):
        return a if flag is True else jnp.where(flag, a, b)

    def both(own, other):
        return jnp.where(
            first,
            jnp.concatenate([own, other], axis=0),
            jnp.concatenate([other, own], axis=0),
        )

    small = [ln1_gain, ln1_bias, b_qv, b_out, ln2_gain, ln2_bias, b_up, b_down]
    sizes = [v.shape[0] for v in small]

    def section(k):
        low = w_qkv[:, k * width : k * width + wide]
        return jnp.where(first, low, w_qkv[:, k * width + skip : k * width + skip + wide])

    w_q, w_k, w_v = section(0), section(1), section(2)
    down_own = lax.dynamic_slice(w_down, (slab * c, 0), (slab, width))
    out_own = lax.dynamic_slice(w_out, (0, skip * c), (part, wide))
    up_cols = w_up.reshape(part, count, 2, slab)
    up_own = lax.dynamic_index_in_dim(up_cols, c, 2, keepdims=False).reshape(part, half_ff)
    up_skip = half_ff // 2 // 128 * 128
    up_wide = half_ff - up_skip
    if grid.split:
        far = grid.far
        mine = jnp.where(lead, w_q, w_v)
        tail = jnp.stack([jnp.pad(v, (0, 2 * wide - v.shape[0])) for v in small])
        lines = grid.lines(
            jnp.concatenate([jnp.concatenate([mine, w_k], axis=1), tail], axis=0)
        )
        up_cut = lambda rep: lax.dynamic_slice(up_own, (0, up_skip * rep), (part, up_wide))
        lines, up_mine, out_own, down_own = hold((lines, up_cut(y), out_own, down_own))
        half_out = grid.gather_all(out_own)
        full_down = grid.gather_all(down_own)
        qkv_near = jnp.stack(lines)
        qkv_next = grid.near_shift(qkv_near, 1)
        up_lines = grid.lines(up_mine)
        qkv_near, qkv_next, up_lines = hold((qkv_near, qkv_next, up_lines))
        qkv_other = grid.swap_rep(
            jnp.stack([qkv_near[:, :part, :wide], qkv_next[:, :part, :wide]])
        )
        up_near = jnp.stack(up_lines)
        up_next = grid.near_shift(up_near, 1)
        spots = jnp.stack(
            grid.spots() + [up_skip * y, (up_wide - up_skip) * (1 - y), up_wide * (1 - y)]
        ).astype(jnp.int32)
        tails = jnp.concatenate([qkv_near[:, part:, : max(sizes)], qkv_next[:, part:, : max(sizes)]])
        chosen = spots[None, :count, None, None] == jnp.arange(count)[:, None, None, None]
        tails = jnp.sum(jnp.where(chosen, tails[None].astype(F32), 0.0), axis=1)
        small_full = [tails[:, i, :size].reshape(-1) for i, size in enumerate(sizes)]
    else:
        small_full = [grid.gather_all(v).astype(F32) for v in small]
        half_out = grid.gather_all(out_own)
        full_up = grid.gather_all(up_own)
        full_down = grid.gather_all(down_own)
    gain_one, shift_one, bias_qv, bias_out, gain_two, shift_two, bias_up, bias_down = small_full

    all_tokens = both(own_tokens, grid.swap_ctx(own_tokens))
    all_cot = both(own_cot, grid.swap_ctx(own_cot))
    inputs = all_tokens.astype(F32)
    scaled_one, _ = moments(inputs)
    normed = (scaled_one * gain_one + shift_one).astype(BF)
    if grid.split:
        qkv_near, qkv_next, qkv_other, up_near, up_next, normed = hold(
            (qkv_near, qkv_next, qkv_other, up_near, up_next, normed)
        )
        full_qkv = assemble(
            spots,
            [qkv_near, qkv_next, qkv_other],
            [(i // far, (i % far,), i, 0, 0, 2 * wide) for i in range(count)]
            + [(2, (i // far, i % far), i, 0, 2 * wide, wide) for i in range(count)],
            (count, part, 3 * wide),
        )
        up_other = grid.swap_rep(jnp.stack([up_near, up_next]))
    else:
        full_qkv = grid.gather_all(jnp.concatenate([w_q, w_k, w_v], axis=1))
    full_qkv = full_qkv.reshape(width, 3 * wide)

    bias_q = lax.dynamic_slice(bias_qv, (skip * c,), (wide,))
    bias_v = lax.dynamic_slice(bias_qv, (width + skip * c,), (wide,))
    bias_row = jnp.concatenate(
        [choose(lead, bias_q, bias_v), jnp.zeros((wide,), F32), choose(lead, bias_v, bias_q)]
    )
    project = (product(full_qkv, normed, 0, 1) + bias_row[:, None]).astype(BF)
    flip = jnp.int32(0) if lead is True else jnp.where(lead, 0, 2).astype(jnp.int32)
    info = jnp.stack([flip, 2 - flip, prefix_len[0], c.astype(jnp.int32)])
    mixed, logs = attend(project, info, heads)
    other_out = grid.swap_ctx(half_out)
    full_out = jnp.concatenate(
        [jnp.where(first, half_out, other_out)[:, :skip], jnp.where(first, other_out, half_out)],
        axis=1,
    )
    bias_up_own = lax.dynamic_index_in_dim(bias_up.reshape(count, 2, slab), c, 1, keepdims=False)
    bias_up_own = bias_up_own.reshape(half_ff)
    own_mixed = mixed.reshape(wide, total_len)
    other_mixed = grid.swap_ctx(own_mixed)
    overlap = wide - skip
    attended = jnp.where(
        first,
        jnp.concatenate([own_mixed, other_mixed[overlap:]], axis=0),
        jnp.concatenate([other_mixed, own_mixed[overlap:]], axis=0),
    )

    middle = inputs + product(attended, full_out, 0, 0) + bias_out
    if grid.split:
        middle, up_other = hold((middle, up_other))
        full_up = assemble(
            spots,
            [up_near, up_next, up_other],
            [(i // far, (i % far,), i, 0, (count,), up_wide) for i in range(count)]
            + [
                (2, (i // far, i % far), i, (count + 1,), (count + 2,), up_skip)
                for i in range(count)
            ],
            (count, part, half_ff),
        ).reshape(width, half_ff)
    scaled_two, inverse_two = moments(middle)
    hidden_in = (scaled_two * gain_two + shift_two).astype(BF)
    pre = product(hidden_in, full_up, 1, 0) + bias_up_own
    cdf = 0.5 + 0.5 * lax.erf(pre * (0.5**0.5))
    activated = (pre * cdf).astype(BF)
    slope = (cdf + pre * jnp.exp(-0.5 * pre * pre) * (0.5 / jnp.pi) ** 0.5).astype(BF)

    own_rows = lambda array: lax.dynamic_slice(array, (rows * c, 0), (rows, array.shape[1]))
    other_rows = lambda array: lax.dynamic_slice(
        array, (rows * (1 - c), 0), (rows, array.shape[1])
    )

    grad_down = product(activated, all_cot, 0, 0).astype(BF)
    full_down, grad_down = hold((full_down, grad_down))
    grad_act = product(all_cot, full_down, 1, 1)
    grad_pre = (grad_act * slope.astype(F32)).astype(BF)
    if grid.split:
        own_down = grid.scatter_all(grad_down)
        grad_cut = lambda rep: lax.dynamic_slice(grad_pre, (0, up_skip * rep), (total_len, up_wide))
        up_sent = product(hidden_in, grad_cut(1 - y), 0, 0).astype(BF)
        up_mine = product(hidden_in, grad_cut(y), 0, 0).astype(BF)
        rows_cube = lambda g: g.reshape(far, grid.near, part, g.shape[1])
        groups = grid.groups()
        up_sent, up_mine = rows_cube(up_sent), rows_cube(up_mine)
        up_sent = [grid.swap_rep(grid.pick_lines(up_sent, steps)) for steps in groups]
    else:
        own_down = grid.scatter_all(grad_down)
        grad_up = product(hidden_in, grad_pre, 0, 0).astype(BF)
    grad_hidden = product(grad_pre, full_up, 1, 1)
    partial_down = product(activated, full_down, 1, 0)
    result = own_rows(partial_down) + grid.swap_ctx(other_rows(partial_down))
    block_out = (own_rows(middle) + result + bias_down).astype(BF).reshape(seqs, rows, width)
    grad_hidden = grad_hidden + grid.swap_ctx(grad_hidden)
    if grid.split:
        grad_hidden, up_mine, up_sent[0], block_out = hold(
            (grad_hidden, up_mine, up_sent[0], block_out)
        )
        merge = lambda i: (
            grid.pick_lines(up_mine, groups[i]).astype(F32) + up_sent[i].astype(F32)
        ).astype(BF)
        up_cubes = [merge(0)]
        up_near = [grid.near_send(up_cubes[0])]
    grad_middle = all_cot.astype(F32) + norm_backward(grad_hidden, scaled_two, inverse_two, gain_two)
    grad_branch = grad_middle.astype(BF)
    if grid.split:
        grad_branch, up_near, up_cubes, block_out = hold(
            (grad_branch, up_near, up_cubes, block_out)
        )
        send_far = lambda i: {
            k: grid.far_shift(grid.line_sum(up_cubes[i], up_near[i], at).astype(BF), k)
            for at, k in enumerate(groups[i])
            if k
        }
        up_far = send_far(0)
    branch_cols = lax.dynamic_slice(grad_branch, (0, skip * c), (total_len, wide))
    grad_wout = product(attended, branch_cols, 1, 0).astype(BF)
    out_rows = lax.dynamic_slice(full_out, (skip * c, 0), (wide, width))
    grad_mixed = product(out_rows, grad_branch, 1, 1).astype(BF).reshape(heads, HD, total_len)
    if grid.split:
        up_sent[1], grad_wout, grad_mixed = hold((up_sent[1], grad_wout, grad_mixed))
        up_cubes.append(merge(1))
        up_near.append(grid.near_send(up_cubes[1]))
        out_cube = rows_cube(grad_wout)
        out_near = grid.near_send(out_cube)
    grad_cube = attend_back(project, info, mixed, grad_mixed, logs, heads)
    grad_project = grad_cube.reshape(3 * wide, total_len)
    qkv_sent = product(normed, grad_project[2 * wide :], 0, 1).astype(BF)
    if grid.split:
        qkv_keys = product(normed, grad_project[wide : 2 * wide], 0, 1).astype(BF)
        qkv_mine = product(normed, grad_project[:wide], 0, 1).astype(BF)
    else:
        qkv_mine = product(normed, grad_project[: 2 * wide], 0, 1).astype(BF)
    if grid.split:
        qkv_sent, qkv_mine, qkv_keys, grad_project, up_near, up_cubes, out_near, out_cube = hold(
            (qkv_sent, qkv_mine, qkv_keys, grad_project, up_near, up_cubes, out_near, out_cube)
        )
        qkv_sent = grid.swap_rep(qkv_sent)
        up_far.update(send_far(1))
        out_far = [
            grid.far_shift(grid.near_sum(out_cube, out_near, k).astype(BF), k)
            for k in range(1, far)
        ]
        key_cube = rows_cube(qkv_keys)
        key_near = grid.near_send(key_cube)
    grad_normed = product(grad_project, full_qkv, 0, 1)
    if grid.split:
        qkv_sent, qkv_mine, key_near, key_cube, grad_normed = hold(
            (qkv_sent, qkv_mine, key_near, key_cube, grad_normed)
        )
        own_down = hold(own_down, qkv_sent)
        down_other = grid.swap_rep(own_down)
        low = qkv_mine.astype(F32) + qkv_sent.astype(F32)
        low_cube = rows_cube(low.astype(BF))
        low_near = grid.near_send(low_cube)
    own_grad = own_rows(grad_normed) + grid.swap_ctx(other_rows(grad_normed))
    own_scaled, own_inverse = moments(own_tokens.astype(F32))
    grad_tokens = own_rows(grad_middle) + norm_backward(own_grad, own_scaled, own_inverse, gain_one)
    grad_tokens = grad_tokens.reshape(seqs, rows, width)

    once = jnp.where(first, 1.0, 0.0).astype(F32)
    spread = lambda values, start, size: lax.dynamic_update_slice(
        jnp.zeros((size,), F32), values, (start,)
    )
    project_sums = jnp.sum(grad_cube.astype(F32), axis=3).reshape(3, wide)
    sums_q = choose(lead, project_sums[0], project_sums[2])
    sums_v = choose(lead, project_sums[2], project_sums[0])
    grad_bias_qv = jnp.concatenate(
        [spread(sums_q, skip * c, width), spread(sums_v, skip * c, width)]
    )
    pre_sums = jnp.sum(grad_pre.astype(F32), axis=0).reshape(count, slab)
    grad_bias_up = lax.dynamic_update_slice(
        jnp.zeros((count, 2, slab), F32), pre_sums[:, None], (0, c, 0)
    )
    vectors = [
        jnp.sum(own_grad * own_scaled, axis=0),
        jnp.sum(own_grad, axis=0),
        grad_bias_qv,
        once * jnp.sum(grad_branch.astype(F32), axis=0),
        once * jnp.sum(grad_hidden * scaled_two, axis=0),
        once * jnp.sum(grad_hidden, axis=0),
        grad_bias_up,
        once * jnp.sum(all_cot.astype(F32), axis=0),
    ]
    table = jnp.concatenate([v.reshape(count, -1) for v in vectors], axis=1)
    table = table + grid.swap_ctx(table)
    table = table + grid.swap_rep(table) if grid.split else lax.psum(table, "rep")

    if grid.split:
        low_near, low_cube, key_near, key_cube, own_grad = hold(
            (low_near, low_cube, key_near, key_cube, own_grad)
        )
        key_far = [
            grid.far_shift(grid.near_sum(key_cube, key_near, k).astype(BF), k)
            for k in range(1, far)
        ]
        up_total = grid.line_sum(up_cubes[1], up_near[1], far - far // 2 - 1)
        for extra in up_far.values():
            up_total += extra.astype(F32)
        out_total = grid.near_sum(out_cube, out_near, 0)
        for extra in out_far:
            out_total += extra.astype(F32)
        pair = jnp.concatenate([up_total.astype(BF), out_total.astype(BF)], axis=1)
        low_far = [
            grid.far_shift(grid.near_sum(low_cube, low_near, k).astype(BF), k)
            for k in range(1, far)
        ]
        pair_other = grid.swap_rep(pair)
        places = jnp.stack([y, c]).astype(jnp.int32)
        out_up, out_wout = finish_pair(
            places,
            (pair, pair_other),
            (grid.swap_ctx(pair), grid.swap_ctx(pair_other)),
            count,
            up_wide,
            skip,
        )
        out_down = finish_down(
            places,
            (own_down, down_other),
            (grid.swap_ctx(own_down), grid.swap_ctx(down_other)),
        )
    else:
        own_down = grid.sum_rep(own_down).astype(BF)
        other_down = grid.swap_ctx(own_down)
        out_down = jnp.where(
            first,
            jnp.concatenate([own_down, other_down], axis=0),
            jnp.concatenate([other_down, own_down], axis=0),
        ).astype(F32)
        own_up = grid.sum_rep(grid.scatter_all(grad_up)).astype(BF)
        other_up = grid.swap_ctx(own_up)
        weave = lambda a, b: jnp.stack(
            [a.reshape(part, count, slab), b.reshape(part, count, slab)], axis=2
        ).reshape(part, ff)
        out_up = weave(
            jnp.where(first, own_up, other_up), jnp.where(first, other_up, own_up)
        ).astype(F32)
        own_wout = grid.sum_rep(grid.scatter_all(grad_wout)).astype(BF)
        other_wout = grid.swap_ctx(own_wout)
        out_wout = jnp.concatenate(
            [
                jnp.where(first, own_wout, other_wout)[:, :skip],
                jnp.where(first, other_wout, own_wout),
            ],
            axis=1,
        ).astype(F32)

    if grid.split:
        keys = grid.near_sum(key_cube, key_near, 0)
        for extra in key_far:
            keys += extra.astype(F32)
        centre = grid.sum_rep(keys).astype(BF)
        low_far, out_up, out_wout, out_down, centre = hold(
            (low_far, out_up, out_wout, out_down, centre)
        )
        mine = grid.near_sum(low_cube, low_near, 0)
        for extra in low_far:
            mine += extra.astype(F32)
        mine = mine.astype(BF)
        other = grid.swap_rep(mine)
        own_sections = [
            jnp.where(lead, mine, other),
            centre,
            jnp.where(lead, other, mine),
        ]
    else:
        own_qkv = [grid.sum_rep(grid.scatter_all(g)).astype(BF) for g in (qkv_mine, qkv_sent)]
        own_sections = [own_qkv[0][:, :wide], own_qkv[0][:, wide:], own_qkv[1]]
    own_qkv = jnp.concatenate(own_sections, axis=1)
    other_qkv = grid.swap_ctx(own_qkv)
    low_qkv = jnp.where(first, own_qkv, other_qkv)
    high_qkv = jnp.where(first, other_qkv, own_qkv)
    pieces = []
    for k in range(3):
        pieces.append(low_qkv[:, k * wide : k * wide + skip])
        pieces.append(high_qkv[:, k * wide : (k + 1) * wide])
    out_qkv = jnp.concatenate(pieces, axis=1).astype(F32)

    summed = grid.scatter(table[:, None, :]).reshape(-1)
    outs, at = [], 0
    for size in sizes:
        outs.append(summed[at : at + size])
        at += size
    return (
        block_out,
        grad_tokens,
        outs[0],
        outs[1],
        out_qkv,
        outs[2],
        out_wout,
        outs[3],
        outs[4],
        outs[5],
        out_up,
        outs[6],
        out_down,
        outs[7],
    )


def solution(mesh):
    placed = (
        P(("fsdp", "rep"), "ctx", None),
        P(("fsdp", "rep")),
        P("fsdp"),
        P("fsdp"),
        P("fsdp", None),
        P("fsdp"),
        P("fsdp", None),
        P("fsdp"),
        P("fsdp"),
        P("fsdp"),
        P("fsdp", None),
        P("fsdp"),
        P("fsdp", None),
        P("fsdp"),
        P(("fsdp", "rep"), "ctx", None),
    )
    return jax.shard_map(
        shards,
        mesh=mesh,
        in_specs=placed,
        out_specs=(
            P(("fsdp", "rep"), "ctx", None),
            P(("fsdp", "rep"), "ctx", None),
            P("fsdp"),
            P("fsdp"),
            P("fsdp", None),
            P("fsdp"),
            P("fsdp", None),
            P("fsdp"),
            P("fsdp"),
            P("fsdp"),
            P("fsdp", None),
            P("fsdp"),
            P("fsdp", None),
            P("fsdp"),
        ),
        check_vma=False,
    )
```
